32 devices in a mesh: parts: 2 (over y), src: 4 (over z), tile: 2 (over x), row: 2 (over core).
Axes of the slice: x: 2, y: 2, z: 4, core: 2. Of those that a mesh axis runs over, the one named last changes fastest.
Arguments:
- mask_windows: float32 [4, 256, 256], P(('parts', 'tile'), ('src', 'row')), parts along dimension 0, may hold values from -4 to 4
- target_windows: float32 [4, 256, 256], P(('parts', 'tile'), ('src', 'row')), parts along dimension 0, may hold values from 0 to 1
- pupil_bands: int32 [24, 128, 2], P(('parts', 'src')), parts along dimension 0, may hold values from 0 to 128, as said below
- pupil_phase: float32 [24, 128, 128], P(('parts', 'src')), parts along dimension 0, may hold values from -3.140625 to 3.140625
- source_weight: float32 [24], P(('parts', 'src')), parts along dimension 0, may hold values from 0.2 to 1
Outputs:
- mask_grad: float32 [4, 256, 256], P(('parts', 'tile'), ('src', 'row')), parts along dimension 0
- source_grad: float32 [24], P(('parts', 'src')), parts along dimension 0
The draws below stay inside these ranges and needn't reach their ends.
There are 2 independent parts, one for each index of `parts`. The reference program is written for one: setup_inputs(seed, part) draws one part's arguments, and reference() takes and returns one part's arrays. A program takes and returns all parts, laid end to end along the dimension named above; each array names one. Nothing has to cross between parts.
Inputs may be any that keep to these rules, and one draw needn't show every extreme that they name: For every source point and frequency row, pupil_bands[s, kx, 0] <= pupil_bands[s, kx, 1]; a row that passes nothing holds (0, 0).
All inputs are finite; a program needn't handle non-finite values.
Results may differ from the reference program's by a relative error of at most 0.00019.
Values sent between devices are 32-bit elements; how exact they have to be, the bound alone decides.
A program may use at most 64 MiB of HBM per device.

```python
import math
import jax
import jax.numpy as jnp
from jax import lax

M = 256
K = 128
OV = 32
S = 12
W = 2


def draw_pupil_bands(key, part):
    reach_max = 3 * K // 16
    radius = 5 * K // 16
    centre = K // 2
    key_rows, key_cols = jax.random.split(jax.random.fold_in(key, 11))
    shift_rows = jax.random.randint(key_rows, (S,), -reach_max, reach_max + 1)
    shift_cols = jax.random.randint(key_cols, (S,), -reach_max, reach_max + 1)
    shift_cols = shift_cols.at[0].set(reach_max)
    freq_index = jnp.arange(K, dtype=jnp.int32)
    dist_rows = freq_index[None, :] - centre - shift_rows[:, None]
    dist_cols = freq_index[None, :] - centre - shift_cols[:, None]
    inside = dist_rows[:, :, None] * dist_rows[:, :, None] + dist_cols[:, None, :] * dist_cols[:, None, :] <= radius * radius
    inside = inside.astype(jnp.int32)
    band_hi = jnp.max(inside * (freq_index[None, None, :] + 1), axis=2)
    band_lo = jnp.where(band_hi > 0, K - jnp.max(inside * (K - freq_index[None, None, :]), axis=2), 0)
    return jnp.stack([band_lo, band_hi], axis=2).astype(jnp.int32)


def levels(rng, shape, shards, low, high):
    def one(dim, shards_of):
        heights = jax.random.uniform(jax.random.fold_in(jax.random.fold_in(rng, 6), dim), (shards_of,), jnp.float32, low / len(shards), high / len(shards))
        return jnp.repeat(jnp.exp(heights), shape[dim] // shards_of).reshape((-1,) + (1,) * (len(shape) - dim - 1))

    factor_of = one(*shards[0])
    for cut in shards[1:]:
        factor_of = factor_of * one(*cut)
    return factor_of


def scatter_about(own_key, extent, deviation, most, cuts=(), kind=jnp.bfloat16):
    drawn = jax.random.normal(own_key, extent, jnp.float32) * deviation
    if len(cuts) > 0:
        drawn = levels(own_key, extent, cuts, -0.22, 0.18) * drawn
    return jnp.clip(drawn, min=-most, max=most).astype(kind)


def setup_inputs(seed: int = 0, part: int = 0) -> dict:
    keys = jax.random.split(jax.random.key(seed), 6)
    part_keys = jax.random.split(jax.random.fold_in(keys[5], part), 6)
    return {
        "mask_windows": scatter_about(part_keys[0], (W, M, M), 1.0, 4.0, ((0, 2), (1, 8)), jnp.float32),
        "target_windows": jnp.clip(1.0 * jax.random.uniform(part_keys[1], (W, M, M), jnp.float32) ** levels(part_keys[1], (W, M, M), ((0, 2), (1, 8)), -0.2, 0.2), 0.0, 1.0),
        "pupil_bands": draw_pupil_bands(jax.random.fold_in(jax.random.fold_in(keys[5], part), 71), part),
        "pupil_phase": jnp.clip(jax.random.uniform(part_keys[3], (S, K, K), jnp.float32, -3.140625, 3.140625), -3.140625, 3.140625),
        "source_weight": jnp.clip(jnp.exp(math.log(1.0) - 1.609438 * jax.random.uniform(part_keys[4], (S,), jnp.float32) ** levels(part_keys[4], (S,), ((0, 4),), -0.2, 0.2)), 0.2, 1.0),
    }


STEEPNESS = 20.0
THRESHOLD = 0.15
LOSS_SCALE = 32.0


def matmul(left_op, right_op):
    return jnp.dot(left_op, right_op, precision=lax.Precision.HIGHEST, preferred_element_type=jnp.float32)


def wave_tables(positions):
    freq_index = jnp.arange(K, dtype=jnp.int32) - K // 2
    phase_index = (freq_index[:, None] * positions[None, :]) % M
    angles = (2.0 * math.pi / M) * phase_index.astype(jnp.float32)
    return jnp.cos(angles), jnp.sin(angles)


def pupil_gate(pupil_bands, pupil_phase):
    freq_cols = jnp.arange(K, dtype=jnp.int32)
    inside = (freq_cols[None, None, :] >= pupil_bands[:, :, 0:1]) & (freq_cols[None, None, :] < pupil_bands[:, :, 1:2])
    passing = inside.astype(jnp.float32)
    return passing * jnp.cos(pupil_phase), passing * jnp.sin(pupil_phase)


def reference(mask_windows, target_windows, pupil_bands, pupil_phase, source_weight):
    cos_tab, sin_tab = wave_tables(jnp.arange(M, dtype=jnp.int32))
    field_scale = 1.0 / (M * K)
    pupil_real, pupil_imag = pupil_gate(pupil_bands, pupil_phase)
    weights = source_weight / S

    def fields(spec_real, spec_imag, pass_real, pass_imag):
        amp_real = pass_real * spec_real - pass_imag * spec_imag
        amp_imag = pass_imag * spec_real + pass_real * spec_imag
        half_real = matmul(amp_real, cos_tab) - matmul(amp_imag, sin_tab)
        half_imag = matmul(amp_real, sin_tab) + matmul(amp_imag, cos_tab)
        field_real = field_scale * (matmul(cos_tab.T, half_real) - matmul(sin_tab.T, half_imag))
        field_imag = field_scale * (matmul(cos_tab.T, half_imag) + matmul(sin_tab.T, half_real))
        return field_real, field_imag

    def one_window(inputs):
        window, goal_window = inputs
        part_real = matmul(window, cos_tab.T)
        part_imag = -matmul(window, sin_tab.T)
        spec_real = matmul(cos_tab, part_real) + matmul(sin_tab, part_imag)
        spec_imag = matmul(cos_tab, part_imag) - matmul(sin_tab, part_real)

        def add_light(totals, source_in):
            pass_real, pass_imag, weight = source_in
            field_real, field_imag = fields(spec_real, spec_imag, pass_real, pass_imag)
            return totals + weight * (field_real * field_real + field_imag * field_imag), None

        intensity = lax.scan(add_light, jnp.zeros((M, M), jnp.float32), (pupil_real, pupil_imag, weights))[0]
        resist = jax.nn.sigmoid(STEEPNESS * (intensity - THRESHOLD))
        cotangent = LOSS_SCALE * (resist - goal_window) * STEEPNESS * resist * (1.0 - resist)

        def add_back(totals, source_in):
            grad_real, grad_imag = totals
            pass_real, pass_imag, weight = source_in
            field_real, field_imag = fields(spec_real, spec_imag, pass_real, pass_imag)
            back_scale = (2.0 * weight) * cotangent
            back_real = back_scale * field_real
            back_imag = back_scale * field_imag
            adj_real = matmul(cos_tab, back_real) + matmul(sin_tab, back_imag)
            adj_imag = matmul(cos_tab, back_imag) - matmul(sin_tab, back_real)
            amp_grad_real = field_scale * (matmul(adj_real, cos_tab.T) + matmul(adj_imag, sin_tab.T))
            amp_grad_imag = field_scale * (matmul(adj_imag, cos_tab.T) - matmul(adj_real, sin_tab.T))
            grad_real = grad_real + pass_real * amp_grad_real + pass_imag * amp_grad_imag
            grad_imag = grad_imag + pass_real * amp_grad_imag - pass_imag * amp_grad_real
            term_value = jnp.sum(cotangent * (field_real * field_real + field_imag * field_imag))
            return (grad_real, grad_imag), term_value

        zero_spec = jnp.zeros((K, K), jnp.float32)
        grads_pair, source_terms = lax.scan(add_back, (zero_spec, zero_spec), (pupil_real, pupil_imag, weights))
        grad_real, grad_imag = grads_pair
        q_one = matmul(grad_real, cos_tab) - matmul(grad_imag, sin_tab)
        q_two = matmul(grad_real, sin_tab) + matmul(grad_imag, cos_tab)
        grad_window = matmul(cos_tab.T, q_one) - matmul(sin_tab.T, q_two)
        return grad_window, source_terms

    grads, source_terms = lax.map(one_window, (mask_windows, target_windows))
    zero_strip = jnp.zeros((1, M, OV), jnp.float32)
    from_below = jnp.concatenate([zero_strip, grads[:-1, :, M - OV:]], axis=0)
    from_above = jnp.concatenate([grads[1:, :, :OV], zero_strip], axis=0)
    middle = jnp.zeros((W, M, M - 2 * OV), jnp.float32)
    mask_grad = grads + jnp.concatenate([from_below, middle, from_above], axis=2)
    source_grad = jnp.sum(source_terms, axis=0) / (S * M * W)
    return mask_grad, source_grad
```

```python
import functools
import math

import jax
import jax.numpy as jnp
import numpy as np
from jax import lax
from jax.experimental import pallas as pl
from jax.experimental.pallas import tpu as pltpu
from jax.sharding import PartitionSpec as P

M = 256
K = 128
OV = 32


STEEPNESS = 20.0
THRESHOLD = 0.15
LOSS_SCALE = 32.0


def with_halo(block, sides, width):
    for axis, dim in sides:
        count = lax.axis_size(axis)
        forward = [(i, i + 1) for i in range(count - 1)]
        backward = [(target, source) for source, target in forward]
        low = lax.ppermute(
            lax.slice_in_dim(block, block.shape[dim] - width, None, axis=dim), axis, forward
        )
        high = lax.ppermute(lax.slice_in_dim(block, 0, width, axis=dim), axis, backward)
        block = jnp.concatenate([low, block, high], axis=dim)
    return block


def matmul(left_op, right_op):
    return lax.dot_general(
        left_op,
        right_op,
        (((1,), (0,)), ((), ())),
        precision=lax.Precision.HIGHEST,
        preferred_element_type=jnp.float32,
    )


def matmul_tn(left_op, right_op):
    return lax.dot_general(
        left_op,
        right_op,
        (((0,), (0,)), ((), ())),
        precision=lax.Precision.HIGHEST,
        preferred_element_type=jnp.float32,
    )


def matmul_nt(left_op, right_op):
    return lax.dot_general(
        left_op,
        right_op,
        (((1,), (1,)), ((), ())),
        precision=lax.Precision.HIGHEST,
        preferred_element_type=jnp.float32,
    )


def wave_tables(positions):
    freq_index = jnp.arange(K, dtype=jnp.int32) - K // 2
    phase_index = freq_index[:, None] * positions[None, :] % M
    angles = 2.0 * math.pi / M * phase_index.astype(jnp.float32)
    return (jnp.cos(angles), jnp.sin(angles))


def shards_plain(mask_windows, target_windows, pupil_bands, pupil_phase, source_weight):
    src_count = lax.axis_size("src")
    tile_count = lax.axis_size("tile")
    row_count = lax.axis_size("row")
    local_x = mask_windows.shape[1]
    per_device = pupil_phase.shape[0]
    sources = per_device * src_count
    field_scale = 1.0 / (M * K)
    src_id = lax.axis_index("src")
    row_id = lax.axis_index("row")
    x_start = (src_id * row_count + row_id) * local_x
    block_starts = (jnp.arange(src_count, dtype=jnp.int32) * row_count + row_id) * local_x
    row_set = (block_starts[:, None] + jnp.arange(local_x, dtype=jnp.int32)[None, :]).reshape(
        src_count * local_x
    )
    cos_all, sin_all = wave_tables(jnp.arange(M, dtype=jnp.int32))
    cos_set, sin_set = wave_tables(row_set)
    cos_own, sin_own = wave_tables(x_start + jnp.arange(local_x, dtype=jnp.int32))
    window = mask_windows[0]
    goal_block = target_windows[0]
    zero_spec = jnp.zeros((K, K), jnp.float32)
    shard_rows = lax.all_gather(window, ("src", "row"), axis=0, tiled=True)
    part_real = matmul_nt(shard_rows, cos_all)
    part_imag = -matmul_nt(shard_rows, sin_all)
    spec_real = matmul(cos_all, part_real) + matmul(sin_all, part_imag)
    spec_imag = matmul(cos_all, part_imag) - matmul(sin_all, part_real)
    freq_cols = jnp.arange(K, dtype=jnp.int32)
    inside = (freq_cols[None, None, :] >= pupil_bands[:, :, 0:1]) & (
        freq_cols[None, None, :] < pupil_bands[:, :, 1:2]
    )
    passing = inside.astype(jnp.float32)
    pupil_real = passing * jnp.cos(pupil_phase)
    pupil_imag = passing * jnp.sin(pupil_phase)
    amp_real = (pupil_real * spec_real - pupil_imag * spec_imag).reshape(per_device * K, K)
    amp_imag = (pupil_imag * spec_real + pupil_real * spec_imag).reshape(per_device * K, K)
    half_real = (matmul(amp_real, cos_all) - matmul(amp_imag, sin_all)).reshape(per_device, K, M)
    half_imag = (matmul(amp_real, sin_all) + matmul(amp_imag, cos_all)).reshape(per_device, K, M)
    weights = source_weight / sources

    def fields(pair_in):
        one_real, one_imag = pair_in
        field_real = field_scale * (matmul_tn(cos_set, one_real) - matmul_tn(sin_set, one_imag))
        field_imag = field_scale * (matmul_tn(cos_set, one_imag) + matmul_tn(sin_set, one_real))
        return (field_real, field_imag)

    stack_real, stack_imag = lax.map(fields, (half_real, half_imag))
    part_real = stack_real
    part_imag = stack_imag
    intensity = lax.psum_scatter(
        jnp.sum(weights[:, None, None] * (part_real * part_real + part_imag * part_imag), axis=0),
        "src",
        scatter_dimension=0,
        tiled=True,
    )
    resist = jax.nn.sigmoid(STEEPNESS * (intensity - THRESHOLD))
    cotangent = LOSS_SCALE * (resist - goal_block) * STEEPNESS * resist * (1.0 - resist)
    cotangent_all = lax.all_gather(cotangent, "src", axis=0, tiled=True)
    source_ids = jnp.arange(per_device, dtype=jnp.int32)

    def add_back(source_id, totals):
        grad_real, grad_imag, source_terms = totals
        field_real = stack_real[source_id]
        field_imag = stack_imag[source_id]
        back_scale = 2.0 * weights[source_id] * cotangent_all
        back_real = back_scale * field_real
        back_imag = back_scale * field_imag
        adj_real = matmul(cos_set, back_real) + matmul(sin_set, back_imag)
        adj_imag = matmul(cos_set, back_imag) - matmul(sin_set, back_real)
        amp_grad_real = field_scale * (matmul_nt(adj_real, cos_all) + matmul_nt(adj_imag, sin_all))
        amp_grad_imag = field_scale * (matmul_nt(adj_imag, cos_all) - matmul_nt(adj_real, sin_all))
        pass_real = pupil_real[source_id]
        pass_imag = pupil_imag[source_id]
        grad_real = grad_real + pass_real * amp_grad_real + pass_imag * amp_grad_imag
        grad_imag = grad_imag + pass_real * amp_grad_imag - pass_imag * amp_grad_real
        term_value = jnp.sum(cotangent_all * (field_real * field_real + field_imag * field_imag))
        source_terms = source_terms + jnp.where(source_ids == source_id, term_value, 0.0)
        return (grad_real, grad_imag, source_terms)

    grad_real, grad_imag, source_terms = lax.fori_loop(
        0, per_device, add_back, (zero_spec, zero_spec, jnp.zeros((per_device,), jnp.float32))
    )
    grad_real, grad_imag = lax.psum((grad_real, grad_imag), ("src", "row"))
    source_sum = lax.psum(source_terms, ("tile", "row"))
    source_grad = source_sum / (sources * M * tile_count)
    q_one = matmul(grad_real, cos_all) - matmul(grad_imag, sin_all)
    q_two = matmul(grad_real, sin_all) + matmul(grad_imag, cos_all)
    grad_block = matmul_tn(cos_own, q_one) - matmul_tn(sin_own, q_two)
    padded = with_halo(grad_block, (("tile", 1),), OV)
    from_below = padded[:, :OV]
    from_above = padded[:, M + OV :]
    middle = jnp.zeros((local_x, M - 2 * OV), jnp.float32)
    grad_block = grad_block + jnp.concatenate([from_below, middle, from_above], axis=1)
    return (grad_block[None], source_grad)


MESH = pl.DeviceIdType.MESH


def pair(values):
    high = values.astype(jnp.bfloat16)
    return high, (values - high.astype(jnp.float32)).astype(jnp.bfloat16)


def dot_pair(left_op, right_op, contract_right=0):
    dims = (((1,), (contract_right,)), ((), ()))

    def one(a, b):
        return lax.dot_general(a, b, dims, preferred_element_type=jnp.float32)

    (left_high, left_low), (right_high, right_low) = left_op, right_op
    return one(left_high, right_high) + (
        one(left_high, right_low) + one(left_low, right_high)
    )


def wave_constants(pixels, freqs, src_count, row_count, local_x):
    freq_index = np.arange(freqs) - freqs // 2
    angles = 2.0 * np.pi / pixels * (np.outer(freq_index, np.arange(pixels)) % pixels)
    cos_tab, sin_tab = np.cos(angles), np.sin(angles)
    wave_y = np.block([[cos_tab, sin_tab], [-sin_tab, cos_tab]])
    sets = []
    for row in range(row_count):
        starts = (np.arange(src_count) * row_count + row) * local_x
        rows = (starts[:, None] + np.arange(local_x)[None, :]).reshape(-1)
        c, s = cos_tab[:, rows], sin_tab[:, rows]
        sets.append(np.block([[c, s], [-s, c]]))
    wave_x = np.stack(sets)
    return wave_y, wave_x, np.ascontiguousarray(wave_x.transpose(0, 2, 1))


def split_constant(values):
    values = values.astype(np.float32)
    high = values.astype(jnp.bfloat16)
    low = (values - high.astype(np.float32)).astype(jnp.bfloat16)
    return np.stack([high, low])


def kernel(
    src_count,
    row_count,
    tile_count,
    wy_ref,
    wx_ref,
    wxt_ref,
    mask_ref,
    goal_ref,
    band_ref,
    phase_ref,
    weight_ref,
    out_ref,
    terms_ref,
    pbuf,
    tbuf,
    fbuf,
    ubuf,
    part_send,
    part_recv,
    cbuf,
    core_send,
    core_recv,
    grad_send,
    grad_recv,
    halo_send,
    halo_recv,
    term_send,
    term_recv,
    mask_ss,
    mask_rs,
    fwd_ss,
    fwd_rs,
    part_ss,
    part_rs,
    cot_ss,
    cot_rs,
    core_ss,
    core_rs,
    grad_ss,
    grad_rs,
    halo_ss,
    halo_rs,
    term_ss,
    term_rs,
):
    part = lax.axis_index("parts")
    src = lax.axis_index("src")
    tile = lax.axis_index("tile")
    row = lax.axis_index("row")
    local_x, pixels = mask_ref.shape[1:]
    per_device, freqs = phase_ref.shape[:2]
    sources = per_device * src_count
    field_scale = 1.0 / (pixels * freqs)
    other_row = 1 - row
    other_tile = 1 - tile
    steps = list(range(1, src_count))

    def ahead(step):
        return lax.rem(src + step, src_count)

    def behind(step):
        return lax.rem(src + src_count - step, src_count)

    def to(src_ref, dst_ref, ss, rs, src_at=src, tile_at=tile, row_at=row):
        return pltpu.make_async_remote_copy(
            src_ref=src_ref,
            dst_ref=dst_ref,
            send_sem=ss,
            recv_sem=rs,
            device_id=(part, src_at, tile_at, row_at),
            device_id_type=MESH,
        )

    barrier = pltpu.get_barrier_semaphore()
    near = [(src, tile, other_row), (src, other_tile, row), (src, other_tile, other_row)]
    peers = [(ahead(step), tile, row) for step in steps] + near
    for src_at, tile_at, row_at in peers:
        pl.semaphore_signal(
            barrier, inc=1, device_id=(part, src_at, tile_at, row_at), device_id_type=MESH
        )

    wy = (wy_ref[0], wy_ref[1])
    wf = (wy_ref[0, :, :pixels], wy_ref[1, :, :pixels])
    own_slot = src * row_count + row
    pbuf[own_slot] = dot_pair(pair(mask_ref[0]), wf, 1)
    pl.semaphore_wait(barrier, len(peers))

    own_block = pbuf.at[own_slot]
    copies = []
    for step in steps:
        copy = to(own_block, own_block, mask_ss.at[step], mask_rs.at[step], src_at=ahead(step))
        copy.start()
        copies.append(copy)
    copy = to(own_block, own_block, fwd_ss.at[0], fwd_rs.at[0], row_at=other_row)
    copy.start()
    copies.append(copy)

    freq_rows = lax.broadcasted_iota(jnp.int32, (freqs, freqs), 0)
    pupils = []
    for one in range(per_device):
        inside = (freq_rows >= band_ref[one, 0:1, :]) & (freq_rows < band_ref[one, 1:2, :])
        passing = jnp.where(inside, 1.0, 0.0).T
        phase = phase_ref[one]
        pupils.append((passing * jnp.cos(phase), passing * jnp.sin(phase)))

    for step in steps:
        block = pbuf.at[behind(step) * row_count + row]
        to(block, block, mask_ss.at[step], mask_rs.at[step], src_at=ahead(step)).wait_recv()
        copy = to(block, block, fwd_ss.at[step], fwd_rs.at[step], row_at=other_row)
        copy.start()
        copies.append(copy)
    for step in range(src_count):
        block = pbuf.at[behind(step) * row_count + other_row]
        to(block, block, fwd_ss.at[step], fwd_rs.at[step], row_at=other_row).wait_recv()

    columns = pair(pbuf[...].reshape(pixels, pixels))
    spectrum = dot_pair(wf, columns)
    spec_real = spectrum[:freqs, :freqs] - spectrum[freqs:, freqs:]
    spec_imag = spectrum[:freqs, freqs:] + spectrum[freqs:, :freqs]

    amps = jnp.concatenate(
        [
            jnp.concatenate([pr * spec_real - pi * spec_imag for pr, pi in pupils], axis=1),
            jnp.concatenate([pi * spec_real + pr * spec_imag for pr, pi in pupils], axis=1),
        ],
        axis=0,
    )
    wxt = (wxt_ref[0, row], wxt_ref[1, row])
    swept = dot_pair(wxt, pair(amps)) * field_scale
    tbuf[...] = swept.reshape(2 * src_count, local_x, per_device * freqs)

    weights = [weight_ref[one] / sources for one in range(per_device)]
    for step in steps + [0]:
        block = ahead(step)
        real, imag = tbuf[block], tbuf[src_count + block]
        rows = jnp.concatenate(
            [
                jnp.concatenate(
                    [
                        real[:, one * freqs : (one + 1) * freqs],
                        imag[:, one * freqs : (one + 1) * freqs],
                    ],
                    axis=1,
                )
                for one in range(per_device)
            ],
            axis=0,
        )
        field = dot_pair(pair(rows), wy)
        fbuf[block] = field
        squares = field[:, :pixels] * field[:, :pixels] + field[:, pixels:] * field[:, pixels:]
        total = weights[0] * squares[:local_x]
        for one in range(1, per_device):
            total = total + weights[one] * squares[one * local_x : (one + 1) * local_x]
        part_send[step] = total
        if step > 0:
            copy = to(
                part_send.at[step],
                part_recv.at[step],
                part_ss.at[step],
                part_rs.at[step],
                src_at=block,
            )
            copy.start()
            copies.append(copy)

    intensity = part_send[0]
    for step in steps:
        to(
            part_send.at[step],
            part_recv.at[step],
            part_ss.at[step],
            part_rs.at[step],
            src_at=ahead(step),
        ).wait_recv()
        intensity = intensity + part_recv[step]

    resist = 1.0 / (1.0 + jnp.exp(-STEEPNESS * (intensity - THRESHOLD)))
    cotangent = LOSS_SCALE * (resist - goal_ref[0]) * STEEPNESS * resist * (1.0 - resist)
    cbuf[src] = cotangent
    for step in steps:
        block = cbuf.at[src]
        copy = to(block, block, cot_ss.at[step], cot_rs.at[step], src_at=ahead(step))
        copy.start()
        copies.append(copy)

    terms = [jnp.zeros((1, pixels), jnp.float32)] * per_device
    for step in [0] + steps:
        block = behind(step)
        if step > 0:
            slot = cbuf.at[block]
            to(slot, slot, cot_ss.at[step], cot_rs.at[step], src_at=ahead(step)).wait_recv()
        light = cbuf[block]
        backs = []
        for one in range(per_device):
            real = fbuf[block, one * local_x : (one + 1) * local_x, :pixels]
            imag = fbuf[block, one * local_x : (one + 1) * local_x, pixels:]
            lit_real, lit_imag = light * real, light * imag
            scale = 2.0 * weights[one]
            backs.append(jnp.concatenate([scale * lit_real, scale * lit_imag], axis=1))
            terms[one] = terms[one] + jnp.sum(
                lit_real * real + lit_imag * imag, axis=0, keepdims=True
            )
        adjoint = dot_pair(pair(jnp.concatenate(backs, axis=0)), wy, 1)
        for one in range(per_device):
            rows = slice(one * local_x, (one + 1) * local_x)
            cols = slice(one * freqs, (one + 1) * freqs)
            ubuf[block, :, cols] = adjoint[rows, :freqs]
            ubuf[src_count + block, :, cols] = adjoint[rows, freqs:]

    term_send[...] = jnp.zeros(term_send.shape, jnp.float32)
    for one in range(per_device):
        term_send[one : one + 1, :] = terms[one][:, :freqs] + terms[one][:, freqs:]
    for index, (src_at, tile_at, row_at) in enumerate(near):
        copy = to(
            term_send,
            term_recv.at[index],
            term_ss.at[index],
            term_rs.at[index],
            tile_at=tile_at,
            row_at=row_at,
        )
        copy.start()
        copies.append(copy)

    wx = (wx_ref[0, row], wx_ref[1, row])
    swept = ubuf[...].reshape(2 * src_count * local_x, per_device * freqs)
    swept = dot_pair(wx, pair(swept)) * field_scale
    grad_real = jnp.zeros((freqs, freqs), jnp.float32)
    grad_imag = grad_real
    for one, (pr, pi) in enumerate(pupils):
        cols = slice(one * freqs, (one + 1) * freqs)
        real, imag = swept[:freqs, cols], swept[freqs:, cols]
        grad_real = grad_real + pr * real + pi * imag
        grad_imag = grad_imag + pr * imag - pi * real
    grads = pair(jnp.concatenate([grad_real, grad_imag], axis=0))

    def rows_of(index):
        swept = dot_pair((wxt_ref[0, index], wxt_ref[1, index]), grads)
        half = src_count * local_x
        swept = jnp.concatenate([swept[:half], swept[half:]], axis=1)
        return swept.reshape(src_count, local_x, 2 * freqs)

    core_send[...] = rows_of(other_row)
    core_copy = to(core_send, core_recv, core_ss, core_rs, row_at=other_row)
    core_copy.start()
    copies.append(core_copy)
    grad_send[...] = rows_of(row)
    core_copy.wait_recv()
    for step in steps:
        block = ahead(step)
        grad_send[block] = grad_send[block] + core_recv[block]
        copy = to(
            grad_send.at[block],
            grad_recv.at[step],
            grad_ss.at[step],
            grad_rs.at[step],
            src_at=block,
        )
        copy.start()
        copies.append(copy)
    total = grad_send[src] + core_recv[src]
    for step in steps:
        to(
            grad_send.at[ahead(step)],
            grad_recv.at[step],
            grad_ss.at[step],
            grad_rs.at[step],
            src_at=ahead(step),
        ).wait_recv()
        total = total + grad_recv[step]
    grad_block = dot_pair(pair(total), wf)

    low, high = grad_block[:, :freqs], grad_block[:, pixels - freqs :]
    halo_send[...] = jnp.where(tile == 0, high, low)
    halo_copy = to(halo_send, halo_recv, halo_ss, halo_rs, tile_at=other_tile)
    halo_copy.start()
    copies.append(halo_copy)

    for index, (src_at, tile_at, row_at) in enumerate(near):
        to(
            term_send,
            term_recv.at[index],
            term_ss.at[index],
            term_rs.at[index],
            tile_at=tile_at,
            row_at=row_at,
        ).wait_recv()
    total = (term_send[...] + term_recv[0]) + (term_recv[1] + term_recv[2])
    total = total / (sources * pixels * tile_count)
    for one in range(per_device):
        terms_ref[one] = jnp.sum(total[one : one + 1, :])

    halo_copy.wait_recv()
    lanes = lax.broadcasted_iota(jnp.int32, (local_x, freqs), 1)
    strip = halo_recv[...]
    from_below = jnp.where(
        (lanes < OV) & (tile == 1), pltpu.roll(strip, OV, axis=1), 0.0
    )
    from_above = jnp.where(
        (lanes >= freqs - OV) & (tile == 0), pltpu.roll(strip, freqs - OV, axis=1), 0.0
    )
    out_ref[0, :, :freqs] = low + from_below
    out_ref[0, :, pixels - freqs :] = high + from_above
    for copy in copies:
        copy.wait_send()


def shards(mask_windows, target_windows, pupil_bands, pupil_phase, source_weight):
    src_count = lax.axis_size("src")
    tile_count = lax.axis_size("tile")
    row_count = lax.axis_size("row")
    local_x, pixels = mask_windows.shape[1:]
    per_device, freqs = pupil_phase.shape[:2]
    fits = row_count == 2 and tile_count == 2 and src_count > 1
    if not fits or local_x % 8 != 0 or freqs % 128 != 0 or pixels != 2 * freqs:
        return shards_plain(
            mask_windows, target_windows, pupil_bands, pupil_phase, source_weight
        )
    tables = [
        split_constant(one)
        for one in wave_constants(pixels, freqs, src_count, row_count, local_x)
    ]
    bands = jnp.transpose(pupil_bands, (0, 2, 1))
    in_vmem = pl.BlockSpec(memory_space=pltpu.VMEM)
    in_smem = pl.BlockSpec(memory_space=pltpu.SMEM)
    f32 = jnp.float32
    block = (local_x, pixels)
    dma = pltpu.SemaphoreType.DMA
    return pl.pallas_call(
        functools.partial(kernel, src_count, row_count, tile_count),
        out_shape=(
            jax.ShapeDtypeStruct(mask_windows.shape, f32),
            jax.ShapeDtypeStruct(source_weight.shape, f32),
        ),
        in_specs=[in_vmem] * 7 + [in_smem],
        out_specs=(in_vmem, in_smem),
        scratch_shapes=[
            pltpu.VMEM((src_count * row_count,) + block, f32),
            pltpu.VMEM((2 * src_count, local_x, per_device * freqs), f32),
            pltpu.VMEM((src_count, per_device * local_x, 2 * pixels), f32),
            pltpu.VMEM((2 * src_count, local_x, per_device * freqs), f32),
        ]
        + [pltpu.VMEM((src_count,) + block, f32)] * 7
        + [
            pltpu.VMEM((local_x, freqs), f32),
            pltpu.VMEM((local_x, freqs), f32),
            pltpu.VMEM((8, freqs), f32),
            pltpu.VMEM((3, 8, freqs), f32),
        ]
        + [dma((src_count,))] * 8
        + [dma(()), dma(())]
        + [dma((src_count,))] * 2
        + [dma(()), dma(())]
        + [dma((3,))] * 2,
        compiler_params=pltpu.CompilerParams(
            collective_id=0, has_side_effects=True, vmem_limit_bytes=48 * 1024 * 1024
        ),
    )(*tables, mask_windows, target_windows, bands, pupil_phase, source_weight)


def solution(mesh):
    return jax.shard_map(
        shards,
        mesh=mesh,
        in_specs=(
            P(("parts", "tile"), ("src", "row"), None),
            P(("parts", "tile"), ("src", "row"), None),
            P(("parts", "src"), None, None),
            P(("parts", "src"), None, None),
            P(("parts", "src")),
        ),
        out_specs=(P(("parts", "tile"), ("src", "row"), None), P(("parts", "src"))),
        check_vma=False,
    )
```

```python
import functools
import math

import jax
import jax.numpy as jnp
import numpy as np
from jax import lax
from jax.experimental import pallas as pl
from jax.experimental.pallas import tpu as pltpu
from jax.sharding import PartitionSpec as P

M = 256
K = 128
OV = 32


STEEPNESS = 20.0
THRESHOLD = 0.15
LOSS_SCALE = 32.0


def with_halo(block, sides, width):
    for axis, dim in sides:
        count = lax.axis_size(axis)
        forward = [(i, i + 1) for i in range(count - 1)]
        backward = [(target, source) for source, target in forward]
        low = lax.ppermute(
            lax.slice_in_dim(block, block.shape[dim] - width, None, axis=dim), axis, forward
        )
        high = lax.ppermute(lax.slice_in_dim(block, 0, width, axis=dim), axis, backward)
        block = jnp.concatenate([low, block, high], axis=dim)
    return block


def matmul(left_op, right_op):
    return lax.dot_general(
        left_op,
        right_op,
        (((1,), (0,)), ((), ())),
        precision=lax.Precision.HIGHEST,
        preferred_element_type=jnp.float32,
    )


def matmul_tn(left_op, right_op):
    return lax.dot_general(
        left_op,
        right_op,
        (((0,), (0,)), ((), ())),
        precision=lax.Precision.HIGHEST,
        preferred_element_type=jnp.float32,
    )


def matmul_nt(left_op, right_op):
    return lax.dot_general(
        left_op,
        right_op,
        (((1,), (1,)), ((), ())),
        precision=lax.Precision.HIGHEST,
        preferred_element_type=jnp.float32,
    )


def wave_tables(positions):
    freq_index = jnp.arange(K, dtype=jnp.int32) - K // 2
    phase_index = freq_index[:, None] * positions[None, :] % M
    angles = 2.0 * math.pi / M * phase_index.astype(jnp.float32)
    return (jnp.cos(angles), jnp.sin(angles))


def shards_plain(mask_windows, target_windows, pupil_bands, pupil_phase, source_weight):
    src_count = lax.axis_size("src")
    tile_count = lax.axis_size("tile")
    row_count = lax.axis_size("row")
    local_x = mask_windows.shape[1]
    per_device = pupil_phase.shape[0]
    sources = per_device * src_count
    field_scale = 1.0 / (M * K)
    src_id = lax.axis_index("src")
    row_id = lax.axis_index("row")
    x_start = (src_id * row_count + row_id) * local_x
    block_starts = (jnp.arange(src_count, dtype=jnp.int32) * row_count + row_id) * local_x
    row_set = (block_starts[:, None] + jnp.arange(local_x, dtype=jnp.int32)[None, :]).reshape(
        src_count * local_x
    )
    cos_all, sin_all = wave_tables(jnp.arange(M, dtype=jnp.int32))
    cos_set, sin_set = wave_tables(row_set)
    cos_own, sin_own = wave_tables(x_start + jnp.arange(local_x, dtype=jnp.int32))
    window = mask_windows[0]
    goal_block = target_windows[0]
    zero_spec = jnp.zeros((K, K), jnp.float32)
    shard_rows = lax.all_gather(window, ("src", "row"), axis=0, tiled=True)
    part_real = matmul_nt(shard_rows, cos_all)
    part_imag = -matmul_nt(shard_rows, sin_all)
    spec_real = matmul(cos_all, part_real) + matmul(sin_all, part_imag)
    spec_imag = matmul(cos_all, part_imag) - matmul(sin_all, part_real)
    freq_cols = jnp.arange(K, dtype=jnp.int32)
    inside = (freq_cols[None, None, :] >= pupil_bands[:, :, 0:1]) & (
        freq_cols[None, None, :] < pupil_bands[:, :, 1:2]
    )
    passing = inside.astype(jnp.float32)
    pupil_real = passing * jnp.cos(pupil_phase)
    pupil_imag = passing * jnp.sin(pupil_phase)
    amp_real = (pupil_real * spec_real - pupil_imag * spec_imag).reshape(per_device * K, K)
    amp_imag = (pupil_imag * spec_real + pupil_real * spec_imag).reshape(per_device * K, K)
    half_real = (matmul(amp_real, cos_all) - matmul(amp_imag, sin_all)).reshape(per_device, K, M)
    half_imag = (matmul(amp_real, sin_all) + matmul(amp_imag, cos_all)).reshape(per_device, K, M)
    weights = source_weight / sources

    def fields(pair_in):
        one_real, one_imag = pair_in
        field_real = field_scale * (matmul_tn(cos_set, one_real) - matmul_tn(sin_set, one_imag))
        field_imag = field_scale * (matmul_tn(cos_set, one_imag) + matmul_tn(sin_set, one_real))
        return (field_real, field_imag)

    stack_real, stack_imag = lax.map(fields, (half_real, half_imag))
    part_real = stack_real
    part_imag = stack_imag
    intensity = lax.psum_scatter(
        jnp.sum(weights[:, None, None] * (part_real * part_real + part_imag * part_imag), axis=0),
        "src",
        scatter_dimension=0,
        tiled=True,
    )
    resist = jax.nn.sigmoid(STEEPNESS * (intensity - THRESHOLD))
    cotangent = LOSS_SCALE * (resist - goal_block) * STEEPNESS * resist * (1.0 - resist)
    cotangent_all = lax.all_gather(cotangent, "src", axis=0, tiled=True)
    source_ids = jnp.arange(per_device, dtype=jnp.int32)

    def add_back(source_id, totals):
        grad_real, grad_imag, source_terms = totals
        field_real = stack_real[source_id]
        field_imag = stack_imag[source_id]
        back_scale = 2.0 * weights[source_id] * cotangent_all
        back_real = back_scale * field_real
        back_imag = back_scale * field_imag
        adj_real = matmul(cos_set, back_real) + matmul(sin_set, back_imag)
        adj_imag = matmul(cos_set, back_imag) - matmul(sin_set, back_real)
        amp_grad_real = field_scale * (matmul_nt(adj_real, cos_all) + matmul_nt(adj_imag, sin_all))
        amp_grad_imag = field_scale * (matmul_nt(adj_imag, cos_all) - matmul_nt(adj_real, sin_all))
        pass_real = pupil_real[source_id]
        pass_imag = pupil_imag[source_id]
        grad_real = grad_real + pass_real * amp_grad_real + pass_imag * amp_grad_imag
        grad_imag = grad_imag + pass_real * amp_grad_imag - pass_imag * amp_grad_real
        term_value = jnp.sum(cotangent_all * (field_real * field_real + field_imag * field_imag))
        source_terms = source_terms + jnp.where(source_ids == source_id, term_value, 0.0)
        return (grad_real, grad_imag, source_terms)

    grad_real, grad_imag, source_terms = lax.fori_loop(
        0, per_device, add_back, (zero_spec, zero_spec, jnp.zeros((per_device,), jnp.float32))
    )
    grad_real, grad_imag = lax.psum((grad_real, grad_imag), ("src", "row"))
    source_sum = lax.psum(source_terms, ("tile", "row"))
    source_grad = source_sum / (sources * M * tile_count)
    q_one = matmul(grad_real, cos_all) - matmul(grad_imag, sin_all)
    q_two = matmul(grad_real, sin_all) + matmul(grad_imag, cos_all)
    grad_block = matmul_tn(cos_own, q_one) - matmul_tn(sin_own, q_two)
    padded = with_halo(grad_block, (("tile", 1),), OV)
    from_below = padded[:, :OV]
    from_above = padded[:, M + OV :]
    middle = jnp.zeros((local_x, M - 2 * OV), jnp.float32)
    grad_block = grad_block + jnp.concatenate([from_below, middle, from_above], axis=1)
    return (grad_block[None], source_grad)


MESH = pl.DeviceIdType.MESH


def pair(values):
    high = values.astype(jnp.bfloat16)
    return high, (values - high.astype(jnp.float32)).astype(jnp.bfloat16)


def dot_pair(left_op, right_op, contract_right=0):
    dims = (((1,), (contract_right,)), ((), ()))

    def one(a, b):
        return lax.dot_general(a, b, dims, preferred_element_type=jnp.float32)

    (left_high, left_low), (right_high, right_low) = left_op, right_op
    return one(left_high, right_high) + (
        one(left_high, right_low) + one(left_low, right_high)
    )


def wave_constants(pixels, freqs, src_count, row_count, local_x):
    freq_index = np.arange(freqs) - freqs // 2
    angles = 2.0 * np.pi / pixels * (np.outer(freq_index, np.arange(pixels)) % pixels)
    cos_tab, sin_tab = np.cos(angles), np.sin(angles)
    wave_y = np.block([[cos_tab, sin_tab], [-sin_tab, cos_tab]])
    sets = []
    for row in range(row_count):
        starts = (np.arange(src_count) * row_count + row) * local_x
        rows = (starts[:, None] + np.arange(local_x)[None, :]).reshape(-1)
        c, s = cos_tab[:, rows], sin_tab[:, rows]
        sets.append(np.block([[c, s], [-s, c]]))
    wave_x = np.stack(sets)
    return wave_y, wave_x, np.ascontiguousarray(wave_x.transpose(0, 2, 1))


def split_constant(values):
    values = values.astype(np.float32)
    high = values.astype(jnp.bfloat16)
    low = (values - high.astype(np.float32)).astype(jnp.bfloat16)
    return np.stack([high, low])


def kernel(
    src_count,
    row_count,
    tile_count,
    wy_hbm,
    wx_hbm,
    wxt_hbm,
    mask_hbm,
    goal_hbm,
    band_hbm,
    phase_hbm,
    weight_hbm,
    out_ref,
    terms_ref,
    wy_ref,
    wx_ref,
    wxt_ref,
    mask_ref,
    goal_ref,
    band_ref,
    phase_ref,
    weight_ref,
    load_sems,
    pbuf,
    tbuf,
    fbuf,
    ubuf,
    part_send,
    part_recv,
    cbuf,
    core_send,
    core_recv,
    grad_send,
    grad_recv,
    halo_send,
    halo_recv,
    term_send,
    term_recv,
    mask_ss,
    mask_rs,
    fwd_ss,
    fwd_rs,
    part_ss,
    part_rs,
    cot_ss,
    cot_rs,
    core_ss,
    core_rs,
    grad_ss,
    grad_rs,
    halo_ss,
    halo_rs,
    term_ss,
    term_rs,
):
    part = lax.axis_index("parts")
    src = lax.axis_index("src")
    tile = lax.axis_index("tile")
    row = lax.axis_index("row")
    local_x, pixels = mask_ref.shape[1:]
    per_device, freqs = phase_ref.shape[:2]
    sources = per_device * src_count
    field_scale = 1.0 / (pixels * freqs)
    loads = {}
    for index, (name, source, target) in enumerate(
        [
            ("mask", mask_hbm, mask_ref),
            ("wy", wy_hbm, wy_ref),
            ("phase", phase_hbm, phase_ref),
            ("band", band_hbm, band_ref),
            ("wxt", wxt_hbm, wxt_ref),
            ("weight", weight_hbm, weight_ref),
            ("goal", goal_hbm, goal_ref),
            ("wx", wx_hbm.at[:, row], wx_ref),
        ]
    ):
        loads[name] = pltpu.make_async_copy(source, target, load_sems.at[index])
        loads[name].start()
    other_row = 1 - row
    other_tile = 1 - tile
    steps = list(range(1, src_count))

    def ahead(step):
        return lax.rem(src + step, src_count)

    def behind(step):
        return lax.rem(src + src_count - step, src_count)

    def to(src_ref, dst_ref, ss, rs, src_at=src, tile_at=tile, row_at=row):
        return pltpu.make_async_remote_copy(
            src_ref=src_ref,
            dst_ref=dst_ref,
            send_sem=ss,
            recv_sem=rs,
            device_id=(part, src_at, tile_at, row_at),
            device_id_type=MESH,
        )

    barrier = pltpu.get_barrier_semaphore()
    near = [(src, tile, other_row), (src, other_tile, row), (src, other_tile, other_row)]
    peers = [(ahead(step), tile, row) for step in steps] + near
    for src_at, tile_at, row_at in peers:
        pl.semaphore_signal(
            barrier, inc=1, device_id=(part, src_at, tile_at, row_at), device_id_type=MESH
        )

    loads["mask"].wait()
    loads["wy"].wait()
    wy = (wy_ref[0], wy_ref[1])
    wf = (wy_ref[0, :, :pixels], wy_ref[1, :, :pixels])
    own_slot = src * row_count + row
    pbuf[own_slot] = dot_pair(pair(mask_ref[0]), wf, 1)
    pl.semaphore_wait(barrier, len(peers))

    own_block = pbuf.at[own_slot]
    copies = []
    for step in steps:
        copy = to(own_block, own_block, mask_ss.at[step], mask_rs.at[step], src_at=ahead(step))
        copy.start()
        copies.append(copy)
    copy = to(own_block, own_block, fwd_ss.at[0], fwd_rs.at[0], row_at=other_row)
    copy.start()
    copies.append(copy)

    loads["phase"].wait()
    loads["band"].wait()
    freq_rows = lax.broadcasted_iota(jnp.int32, (freqs, freqs), 0)
    pupils = []
    for one in range(per_device):
        inside = (freq_rows >= band_ref[one, 0:1, :]) & (freq_rows < band_ref[one, 1:2, :])
        passing = jnp.where(inside, 1.0, 0.0).T
        phase = phase_ref[one]
        pupils.append((passing * jnp.cos(phase), passing * jnp.sin(phase)))

    for name in ("wxt", "weight", "goal", "wx"):
        loads[name].wait()
    for step in steps:
        block = pbuf.at[behind(step) * row_count + row]
        to(block, block, mask_ss.at[step], mask_rs.at[step], src_at=ahead(step)).wait_recv()
        copy = to(block, block, fwd_ss.at[step], fwd_rs.at[step], row_at=other_row)
        copy.start()
        copies.append(copy)
    for step in range(src_count):
        block = pbuf.at[behind(step) * row_count + other_row]
        to(block, block, fwd_ss.at[step], fwd_rs.at[step], row_at=other_row).wait_recv()

    columns = pair(pbuf[...].reshape(pixels, pixels))
    spectrum = dot_pair(wf, columns)
    spec_real = spectrum[:freqs, :freqs] - spectrum[freqs:, freqs:]
    spec_imag = spectrum[:freqs, freqs:] + spectrum[freqs:, :freqs]

    amps = jnp.concatenate(
        [
            jnp.concatenate([pr * spec_real - pi * spec_imag for pr, pi in pupils], axis=1),
            jnp.concatenate([pi * spec_real + pr * spec_imag for pr, pi in pupils], axis=1),
        ],
        axis=0,
    )
    wxt = (wxt_ref[0, row], wxt_ref[1, row])
    swept = dot_pair(wxt, pair(amps)) * field_scale
    tbuf[...] = swept.reshape(2 * src_count, local_x, per_device * freqs)

    weights = [weight_ref[one] / sources for one in range(per_device)]
    for step in steps + [0]:
        block = ahead(step)
        real, imag = tbuf[block], tbuf[src_count + block]
        rows = jnp.concatenate(
            [
                jnp.concatenate(
                    [
                        real[:, one * freqs : (one + 1) * freqs],
                        imag[:, one * freqs : (one + 1) * freqs],
                    ],
                    axis=1,
                )
                for one in range(per_device)
            ],
            axis=0,
        )
        field = dot_pair(pair(rows), wy)
        fbuf[block] = field
        squares = field[:, :pixels] * field[:, :pixels] + field[:, pixels:] * field[:, pixels:]
        total = weights[0] * squares[:local_x]
        for one in range(1, per_device):
            total = total + weights[one] * squares[one * local_x : (one + 1) * local_x]
        part_send[step] = total
        if step > 0:
            copy = to(
                part_send.at[step],
                part_recv.at[step],
                part_ss.at[step],
                part_rs.at[step],
                src_at=block,
            )
            copy.start()
            copies.append(copy)

    intensity = part_send[0]
    for step in steps:
        to(
            part_send.at[step],
            part_recv.at[step],
            part_ss.at[step],
            part_rs.at[step],
            src_at=ahead(step),
        ).wait_recv()
        intensity = intensity + part_recv[step]

    resist = 1.0 / (1.0 + jnp.exp(-STEEPNESS * (intensity - THRESHOLD)))
    cotangent = LOSS_SCALE * (resist - goal_ref[0]) * STEEPNESS * resist * (1.0 - resist)
    cbuf[src] = cotangent
    for step in steps:
        block = cbuf.at[src]
        copy = to(block, block, cot_ss.at[step], cot_rs.at[step], src_at=ahead(step))
        copy.start()
        copies.append(copy)

    terms = [jnp.zeros((1, pixels), jnp.float32)] * per_device
    for step in [0] + steps:
        block = behind(step)
        if step > 0:
            slot = cbuf.at[block]
            to(slot, slot, cot_ss.at[step], cot_rs.at[step], src_at=ahead(step)).wait_recv()
        light = cbuf[block]
        backs = []
        for one in range(per_device):
            real = fbuf[block, one * local_x : (one + 1) * local_x, :pixels]
            imag = fbuf[block, one * local_x : (one + 1) * local_x, pixels:]
            lit_real, lit_imag = light * real, light * imag
            scale = 2.0 * weights[one]
            backs.append(jnp.concatenate([scale * lit_real, scale * lit_imag], axis=1))
            terms[one] = terms[one] + jnp.sum(
                lit_real * real + lit_imag * imag, axis=0, keepdims=True
            )
        adjoint = dot_pair(pair(jnp.concatenate(backs, axis=0)), wy, 1)
        for one in range(per_device):
            rows = slice(one * local_x, (one + 1) * local_x)
            cols = slice(one * freqs, (one + 1) * freqs)
            ubuf[block, :, cols] = adjoint[rows, :freqs]
            ubuf[src_count + block, :, cols] = adjoint[rows, freqs:]

    term_send[...] = jnp.zeros(term_send.shape, jnp.float32)
    for one in range(per_device):
        term_send[one : one + 1, :] = terms[one][:, :freqs] + terms[one][:, freqs:]
    for index, (src_at, tile_at, row_at) in enumerate(near):
        copy = to(
            term_send,
            term_recv.at[index],
            term_ss.at[index],
            term_rs.at[index],
            tile_at=tile_at,
            row_at=row_at,
        )
        copy.start()
        copies.append(copy)

    wx = (wx_ref[0], wx_ref[1])
    swept = ubuf[...].reshape(2 * src_count * local_x, per_device * freqs)
    swept = dot_pair(wx, pair(swept)) * field_scale
    grad_real = jnp.zeros((freqs, freqs), jnp.float32)
    grad_imag = grad_real
    for one, (pr, pi) in enumerate(pupils):
        cols = slice(one * freqs, (one + 1) * freqs)
        real, imag = swept[:freqs, cols], swept[freqs:, cols]
        grad_real = grad_real + pr * real + pi * imag
        grad_imag = grad_imag + pr * imag - pi * real
    grads = pair(jnp.concatenate([grad_real, grad_imag], axis=0))

    def rows_of(index):
        swept = dot_pair((wxt_ref[0, index], wxt_ref[1, index]), grads)
        half = src_count * local_x
        swept = jnp.concatenate([swept[:half], swept[half:]], axis=1)
        return swept.reshape(src_count, local_x, 2 * freqs)

    core_send[...] = rows_of(other_row)
    core_copy = to(core_send, core_recv, core_ss, core_rs, row_at=other_row)
    core_copy.start()
    copies.append(core_copy)
    grad_send[...] = rows_of(row)
    core_copy.wait_recv()
    for step in steps:
        block = ahead(step)
        grad_send[block] = grad_send[block] + core_recv[block]
        copy = to(
            grad_send.at[block],
            grad_recv.at[step],
            grad_ss.at[step],
            grad_rs.at[step],
            src_at=block,
        )
        copy.start()
        copies.append(copy)
    total = grad_send[src] + core_recv[src]
    for step in steps:
        to(
            grad_send.at[ahead(step)],
            grad_recv.at[step],
            grad_ss.at[step],
            grad_rs.at[step],
            src_at=ahead(step),
        ).wait_recv()
        total = total + grad_recv[step]
    grad_block = dot_pair(pair(total), wf)

    low, high = grad_block[:, :freqs], grad_block[:, pixels - freqs :]
    halo_send[...] = jnp.where(tile == 0, high, low)
    halo_copy = to(halo_send, halo_recv, halo_ss, halo_rs, tile_at=other_tile)
    halo_copy.start()
    copies.append(halo_copy)

    for index, (src_at, tile_at, row_at) in enumerate(near):
        to(
            term_send,
            term_recv.at[index],
            term_ss.at[index],
            term_rs.at[index],
            tile_at=tile_at,
            row_at=row_at,
        ).wait_recv()
    total = (term_send[...] + term_recv[0]) + (term_recv[1] + term_recv[2])
    total = total / (sources * pixels * tile_count)
    for one in range(per_device):
        terms_ref[one] = jnp.sum(total[one : one + 1, :])

    halo_copy.wait_recv()
    lanes = lax.broadcasted_iota(jnp.int32, (local_x, freqs), 1)
    strip = halo_recv[...]
    from_below = jnp.where(
        (lanes < OV) & (tile == 1), pltpu.roll(strip, OV, axis=1), 0.0
    )
    from_above = jnp.where(
        (lanes >= freqs - OV) & (tile == 0), pltpu.roll(strip, freqs - OV, axis=1), 0.0
    )
    out_ref[0, :, :freqs] = low + from_below
    out_ref[0, :, pixels - freqs :] = high + from_above
    for copy in copies:
        copy.wait_send()


def shards(mask_windows, target_windows, pupil_bands, pupil_phase, source_weight):
    src_count = lax.axis_size("src")
    tile_count = lax.axis_size("tile")
    row_count = lax.axis_size("row")
    local_x, pixels = mask_windows.shape[1:]
    per_device, freqs = pupil_phase.shape[:2]
    fits = row_count == 2 and tile_count == 2 and src_count > 1
    if not fits or local_x % 8 != 0 or freqs % 128 != 0 or pixels != 2 * freqs:
        return shards_plain(
            mask_windows, target_windows, pupil_bands, pupil_phase, source_weight
        )
    tables = [
        split_constant(one)
        for one in wave_constants(pixels, freqs, src_count, row_count, local_x)
    ]
    bands = jnp.transpose(pupil_bands, (0, 2, 1))
    in_vmem = pl.BlockSpec(memory_space=pltpu.VMEM)
    in_smem = pl.BlockSpec(memory_space=pltpu.SMEM)
    f32 = jnp.float32
    block = (local_x, pixels)
    dma = pltpu.SemaphoreType.DMA
    return pl.pallas_call(
        functools.partial(kernel, src_count, row_count, tile_count),
        out_shape=(
            jax.ShapeDtypeStruct(mask_windows.shape, f32),
            jax.ShapeDtypeStruct(source_weight.shape, f32),
        ),
        in_specs=[pl.BlockSpec(memory_space=pltpu.HBM)] * 8,
        out_specs=(in_vmem, in_smem),
        scratch_shapes=[
            pltpu.VMEM(tables[0].shape, tables[0].dtype),
            pltpu.VMEM(tables[1].shape[:1] + tables[1].shape[2:], tables[1].dtype),
            pltpu.VMEM(tables[2].shape, tables[2].dtype),
            pltpu.VMEM(mask_windows.shape, f32),
            pltpu.VMEM(target_windows.shape, f32),
            pltpu.VMEM(bands.shape, bands.dtype),
            pltpu.VMEM(pupil_phase.shape, f32),
            pltpu.SMEM(source_weight.shape, f32),
            dma((8,)),
            pltpu.VMEM((src_count * row_count,) + block, f32),
            pltpu.VMEM((2 * src_count, local_x, per_device * freqs), f32),
            pltpu.VMEM((src_count, per_device * local_x, 2 * pixels), f32),
            pltpu.VMEM((2 * src_count, local_x, per_device * freqs), f32),
        ]
        + [pltpu.VMEM((src_count,) + block, f32)] * 7
        + [
            pltpu.VMEM((local_x, freqs), f32),
            pltpu.VMEM((local_x, freqs), f32),
            pltpu.VMEM((8, freqs), f32),
            pltpu.VMEM((3, 8, freqs), f32),
        ]
        + [dma((src_count,))] * 8
        + [dma(()), dma(())]
        + [dma((src_count,))] * 2
        + [dma(()), dma(())]
        + [dma((3,))] * 2,
        compiler_params=pltpu.CompilerParams(
            collective_id=0, has_side_effects=True, vmem_limit_bytes=63 * 1024 * 1024
        ),
    )(*tables, mask_windows, target_windows, bands, pupil_phase, source_weight)


def solution(mesh):
    return jax.shard_map(
        shards,
        mesh=mesh,
        in_specs=(
            P(("parts", "tile"), ("src", "row"), None),
            P(("parts", "tile"), ("src", "row"), None),
            P(("parts", "src"), None, None),
            P(("parts", "src"), None, None),
            P(("parts", "src")),
        ),
        out_specs=(P(("parts", "tile"), ("src", "row"), None), P(("parts", "src"))),
        check_vma=False,
    )
```

```python
import functools
import math

import jax
import jax.numpy as jnp
import numpy as np
from jax import lax
from jax.experimental import pallas as pl
from jax.experimental.pallas import tpu as pltpu
from jax.sharding import PartitionSpec as P

M = 256
K = 128
OV = 32


STEEPNESS = 20.0
THRESHOLD = 0.15
LOSS_SCALE = 32.0


def with_halo(block, sides, width):
    for axis, dim in sides:
        count = lax.axis_size(axis)
        forward = [(i, i + 1) for i in range(count - 1)]
        backward = [(target, source) for source, target in forward]
        low = lax.ppermute(
            lax.slice_in_dim(block, block.shape[dim] - width, None, axis=dim), axis, forward
        )
        high = lax.ppermute(lax.slice_in_dim(block, 0, width, axis=dim), axis, backward)
        block = jnp.concatenate([low, block, high], axis=dim)
    return block


def matmul(left_op, right_op):
    return lax.dot_general(
        left_op,
        right_op,
        (((1,), (0,)), ((), ())),
        precision=lax.Precision.HIGHEST,
        preferred_element_type=jnp.float32,
    )


def matmul_tn(left_op, right_op):
    return lax.dot_general(
        left_op,
        right_op,
        (((0,), (0,)), ((), ())),
        precision=lax.Precision.HIGHEST,
        preferred_element_type=jnp.float32,
    )


def matmul_nt(left_op, right_op):
    return lax.dot_general(
        left_op,
        right_op,
        (((1,), (1,)), ((), ())),
        precision=lax.Precision.HIGHEST,
        preferred_element_type=jnp.float32,
    )


def wave_tables(positions):
    freq_index = jnp.arange(K, dtype=jnp.int32) - K // 2
    phase_index = freq_index[:, None] * positions[None, :] % M
    angles = 2.0 * math.pi / M * phase_index.astype(jnp.float32)
    return (jnp.cos(angles), jnp.sin(angles))


def shards_plain(mask_windows, target_windows, pupil_bands, pupil_phase, source_weight):
    src_count = lax.axis_size("src")
    tile_count = lax.axis_size("tile")
    row_count = lax.axis_size("row")
    local_x = mask_windows.shape[1]
    per_device = pupil_phase.shape[0]
    sources = per_device * src_count
    field_scale = 1.0 / (M * K)
    src_id = lax.axis_index("src")
    row_id = lax.axis_index("row")
    x_start = (src_id * row_count + row_id) * local_x
    block_starts = (jnp.arange(src_count, dtype=jnp.int32) * row_count + row_id) * local_x
    row_set = (block_starts[:, None] + jnp.arange(local_x, dtype=jnp.int32)[None, :]).reshape(
        src_count * local_x
    )
    cos_all, sin_all = wave_tables(jnp.arange(M, dtype=jnp.int32))
    cos_set, sin_set = wave_tables(row_set)
    cos_own, sin_own = wave_tables(x_start + jnp.arange(local_x, dtype=jnp.int32))
    window = mask_windows[0]
    goal_block = target_windows[0]
    zero_spec = jnp.zeros((K, K), jnp.float32)
    shard_rows = lax.all_gather(window, ("src", "row"), axis=0, tiled=True)
    part_real = matmul_nt(shard_rows, cos_all)
    part_imag = -matmul_nt(shard_rows, sin_all)
    spec_real = matmul(cos_all, part_real) + matmul(sin_all, part_imag)
    spec_imag = matmul(cos_all, part_imag) - matmul(sin_all, part_real)
    freq_cols = jnp.arange(K, dtype=jnp.int32)
    inside = (freq_cols[None, None, :] >= pupil_bands[:, :, 0:1]) & (
        freq_cols[None, None, :] < pupil_bands[:, :, 1:2]
    )
    passing = inside.astype(jnp.float32)
    pupil_real = passing * jnp.cos(pupil_phase)
    pupil_imag = passing * jnp.sin(pupil_phase)
    amp_real = (pupil_real * spec_real - pupil_imag * spec_imag).reshape(per_device * K, K)
    amp_imag = (pupil_imag * spec_real + pupil_real * spec_imag).reshape(per_device * K, K)
    half_real = (matmul(amp_real, cos_all) - matmul(amp_imag, sin_all)).reshape(per_device, K, M)
    half_imag = (matmul(amp_real, sin_all) + matmul(amp_imag, cos_all)).reshape(per_device, K, M)
    weights = source_weight / sources

    def fields(pair_in):
        one_real, one_imag = pair_in
        field_real = field_scale * (matmul_tn(cos_set, one_real) - matmul_tn(sin_set, one_imag))
        field_imag = field_scale * (matmul_tn(cos_set, one_imag) + matmul_tn(sin_set, one_real))
        return (field_real, field_imag)

    stack_real, stack_imag = lax.map(fields, (half_real, half_imag))
    part_real = stack_real
    part_imag = stack_imag
    intensity = lax.psum_scatter(
        jnp.sum(weights[:, None, None] * (part_real * part_real + part_imag * part_imag), axis=0),
        "src",
        scatter_dimension=0,
        tiled=True,
    )
    resist = jax.nn.sigmoid(STEEPNESS * (intensity - THRESHOLD))
    cotangent = LOSS_SCALE * (resist - goal_block) * STEEPNESS * resist * (1.0 - resist)
    cotangent_all = lax.all_gather(cotangent, "src", axis=0, tiled=True)
    source_ids = jnp.arange(per_device, dtype=jnp.int32)

    def add_back(source_id, totals):
        grad_real, grad_imag, source_terms = totals
        field_real = stack_real[source_id]
        field_imag = stack_imag[source_id]
        back_scale = 2.0 * weights[source_id] * cotangent_all
        back_real = back_scale * field_real
        back_imag = back_scale * field_imag
        adj_real = matmul(cos_set, back_real) + matmul(sin_set, back_imag)
        adj_imag = matmul(cos_set, back_imag) - matmul(sin_set, back_real)
        amp_grad_real = field_scale * (matmul_nt(adj_real, cos_all) + matmul_nt(adj_imag, sin_all))
        amp_grad_imag = field_scale * (matmul_nt(adj_imag, cos_all) - matmul_nt(adj_real, sin_all))
        pass_real = pupil_real[source_id]
        pass_imag = pupil_imag[source_id]
        grad_real = grad_real + pass_real * amp_grad_real + pass_imag * amp_grad_imag
        grad_imag = grad_imag + pass_real * amp_grad_imag - pass_imag * amp_grad_real
        term_value = jnp.sum(cotangent_all * (field_real * field_real + field_imag * field_imag))
        source_terms = source_terms + jnp.where(source_ids == source_id, term_value, 0.0)
        return (grad_real, grad_imag, source_terms)

    grad_real, grad_imag, source_terms = lax.fori_loop(
        0, per_device, add_back, (zero_spec, zero_spec, jnp.zeros((per_device,), jnp.float32))
    )
    grad_real, grad_imag = lax.psum((grad_real, grad_imag), ("src", "row"))
    source_sum = lax.psum(source_terms, ("tile", "row"))
    source_grad = source_sum / (sources * M * tile_count)
    q_one = matmul(grad_real, cos_all) - matmul(grad_imag, sin_all)
    q_two = matmul(grad_real, sin_all) + matmul(grad_imag, cos_all)
    grad_block = matmul_tn(cos_own, q_one) - matmul_tn(sin_own, q_two)
    padded = with_halo(grad_block, (("tile", 1),), OV)
    from_below = padded[:, :OV]
    from_above = padded[:, M + OV :]
    middle = jnp.zeros((local_x, M - 2 * OV), jnp.float32)
    grad_block = grad_block + jnp.concatenate([from_below, middle, from_above], axis=1)
    return (grad_block[None], source_grad)


MESH = pl.DeviceIdType.MESH


def pair(values):
    high = values.astype(jnp.bfloat16)
    return high, (values - high.astype(jnp.float32)).astype(jnp.bfloat16)


def dot_pair(left_op, right_op, contract_right=0):
    dims = (((1,), (contract_right,)), ((), ()))

    def one(a, b):
        return lax.dot_general(a, b, dims, preferred_element_type=jnp.float32)

    (left_high, left_low), (right_high, right_low) = left_op, right_op
    return one(left_high, right_high) + (
        one(left_high, right_low) + one(left_low, right_high)
    )


def wave_constants(pixels, freqs, src_count, row_count, local_x):
    freq_index = np.arange(freqs) - freqs // 2
    angles = 2.0 * np.pi / pixels * (np.outer(freq_index, np.arange(pixels)) % pixels)
    cos_tab, sin_tab = np.cos(angles), np.sin(angles)
    wave_y = np.block([[cos_tab, sin_tab], [-sin_tab, cos_tab]])
    sets = []
    for row in range(row_count):
        starts = (np.arange(src_count) * row_count + row) * local_x
        rows = (starts[:, None] + np.arange(local_x)[None, :]).reshape(-1)
        c, s = cos_tab[:, rows], sin_tab[:, rows]
        sets.append(np.block([[c, s], [-s, c]]))
    wave_x = np.stack(sets)
    return wave_y, wave_x, np.ascontiguousarray(wave_x.transpose(0, 2, 1))


def split_constant(values):
    values = values.astype(np.float32)
    high = values.astype(jnp.bfloat16)
    low = (values - high.astype(np.float32)).astype(jnp.bfloat16)
    return np.stack([high, low])


def kernel(
    src_count,
    row_count,
    tile_count,
    wy_hbm,
    wx_hbm,
    wxt_hbm,
    mask_hbm,
    goal_hbm,
    band_hbm,
    phase_hbm,
    weight_hbm,
    out_ref,
    terms_ref,
    wy_ref,
    wx_ref,
    wxt_ref,
    mask_ref,
    goal_ref,
    band_ref,
    phase_ref,
    weight_ref,
    load_sems,
    pbuf,
    tbuf,
    fbuf,
    ubuf,
    part_send,
    part_recv,
    cbuf,
    core_send,
    core_recv,
    grad_send,
    grad_recv,
    halo_send,
    halo_recv,
    term_send,
    term_recv,
    mask_ss,
    mask_rs,
    fwd_ss,
    fwd_rs,
    part_ss,
    part_rs,
    cot_ss,
    cot_rs,
    core_ss,
    core_rs,
    grad_ss,
    grad_rs,
    halo_ss,
    halo_rs,
    term_ss,
    term_rs,
):
    part = lax.axis_index("parts")
    src = lax.axis_index("src")
    tile = lax.axis_index("tile")
    row = lax.axis_index("row")
    local_x, pixels = mask_ref.shape[1:]
    per_device, freqs = phase_ref.shape[:2]
    sources = per_device * src_count
    field_scale = 1.0 / (pixels * freqs)
    loads = {}
    for index, (name, source, target) in enumerate(
        [
            ("mask", mask_hbm, mask_ref),
            ("wy", wy_hbm, wy_ref),
            ("phase", phase_hbm, phase_ref),
            ("band", band_hbm, band_ref),
            ("wxt", wxt_hbm, wxt_ref),
            ("weight", weight_hbm, weight_ref),
            ("goal", goal_hbm, goal_ref),
            ("wx", wx_hbm.at[:, row], wx_ref),
        ]
    ):
        loads[name] = pltpu.make_async_copy(source, target, load_sems.at[index])
        loads[name].start()
    other_row = 1 - row
    other_tile = 1 - tile
    last = src_count - 1

    def far(step):
        up = last - src
        side = lax.div(up + last - step, src_count)
        return side * (last - step) + (1 - side) * (step - up)

    far_first = [far(step) for step in range(last)]
    near_first = far_first[::-1]

    def to(src_ref, dst_ref, ss, rs, src_at=src, tile_at=tile, row_at=row):
        return pltpu.make_async_remote_copy(
            src_ref=src_ref,
            dst_ref=dst_ref,
            send_sem=ss,
            recv_sem=rs,
            device_id=(part, src_at, tile_at, row_at),
            device_id_type=MESH,
        )

    barrier = pltpu.get_barrier_semaphore()
    near = [(src, tile, other_row), (src, other_tile, row), (src, other_tile, other_row)]
    peers = [(peer, at, row) for peer in far_first for at in (tile, other_tile)] + near
    for src_at, tile_at, row_at in peers:
        pl.semaphore_signal(
            barrier, inc=1, device_id=(part, src_at, tile_at, row_at), device_id_type=MESH
        )

    loads["mask"].wait()
    loads["wy"].wait()
    wy = (wy_ref[0], wy_ref[1])
    wf = (wy_ref[0, :, :pixels], wy_ref[1, :, :pixels])
    own_slot = src * row_count + row
    pbuf[own_slot] = dot_pair(pair(mask_ref[0]), wf, 1)
    pl.semaphore_wait(barrier, len(peers))

    own_block = pbuf.at[own_slot]
    copies = []
    for peer in far_first:
        copy = to(own_block, own_block, mask_ss.at[peer], mask_rs.at[src], src_at=peer)
        copy.start()
        copies.append(copy)
    copy = to(own_block, own_block, fwd_ss.at[src], fwd_rs.at[src], row_at=other_row)
    copy.start()
    copies.append(copy)

    loads["phase"].wait()
    loads["band"].wait()
    freq_rows = lax.broadcasted_iota(jnp.int32, (freqs, freqs), 0)
    pupils = []
    for one in range(per_device):
        inside = (freq_rows >= band_ref[one, 0:1, :]) & (freq_rows < band_ref[one, 1:2, :])
        passing = jnp.where(inside, 1.0, 0.0).T
        phase = phase_ref[one]
        pupils.append((passing * jnp.cos(phase), passing * jnp.sin(phase)))

    for name in ("wxt", "weight", "goal", "wx"):
        loads[name].wait()
    for peer in near_first:
        block = pbuf.at[peer * row_count + row]
        to(block, block, mask_ss.at[peer], mask_rs.at[peer], src_at=peer).wait_recv()
        copy = to(block, block, fwd_ss.at[peer], fwd_rs.at[peer], row_at=other_row)
        copy.start()
        copies.append(copy)
    for peer in [src] + near_first:
        block = pbuf.at[peer * row_count + other_row]
        to(block, block, fwd_ss.at[peer], fwd_rs.at[peer], row_at=other_row).wait_recv()

    columns = pair(pbuf[...].reshape(pixels, pixels))
    spectrum = dot_pair(wf, columns)
    spec_real = spectrum[:freqs, :freqs] - spectrum[freqs:, freqs:]
    spec_imag = spectrum[:freqs, freqs:] + spectrum[freqs:, :freqs]

    amps = jnp.concatenate(
        [
            jnp.concatenate([pr * spec_real - pi * spec_imag for pr, pi in pupils], axis=1),
            jnp.concatenate([pi * spec_real + pr * spec_imag for pr, pi in pupils], axis=1),
        ],
        axis=0,
    )
    wxt = (wxt_ref[0, row], wxt_ref[1, row])
    swept = dot_pair(wxt, pair(amps)) * field_scale
    tbuf[...] = swept.reshape(2 * src_count, local_x, per_device * freqs)

    weights = [weight_ref[one] / sources for one in range(per_device)]
    for block in far_first + [src]:
        real, imag = tbuf[block], tbuf[src_count + block]
        rows = jnp.concatenate(
            [
                jnp.concatenate(
                    [
                        real[:, one * freqs : (one + 1) * freqs],
                        imag[:, one * freqs : (one + 1) * freqs],
                    ],
                    axis=1,
                )
                for one in range(per_device)
            ],
            axis=0,
        )
        field = dot_pair(pair(rows), wy)
        fbuf[block] = field
        squares = field[:, :pixels] * field[:, :pixels] + field[:, pixels:] * field[:, pixels:]
        total = weights[0] * squares[:local_x]
        for one in range(1, per_device):
            total = total + weights[one] * squares[one * local_x : (one + 1) * local_x]
        if block is not src:
            part_send[block] = total
            copy = to(
                part_send.at[block],
                part_recv.at[src],
                part_ss.at[block],
                part_rs.at[src],
                src_at=block,
            )
            copy.start()
            copies.append(copy)

    intensity = total
    for peer in near_first:
        to(
            part_send.at[peer],
            part_recv.at[peer],
            part_ss.at[peer],
            part_rs.at[peer],
            src_at=peer,
        ).wait_recv()
        intensity = intensity + part_recv[peer]

    resist = 1.0 / (1.0 + jnp.exp(-STEEPNESS * (intensity - THRESHOLD)))
    cotangent = LOSS_SCALE * (resist - goal_ref[0]) * STEEPNESS * resist * (1.0 - resist)
    cbuf[src] = cotangent
    for peer in far_first:
        block = cbuf.at[src]
        copy = to(block, block, cot_ss.at[peer], cot_rs.at[src], src_at=peer)
        copy.start()
        copies.append(copy)

    terms = [jnp.zeros((1, pixels), jnp.float32)] * per_device
    for block in [src] + near_first:
        if block is not src:
            slot = cbuf.at[block]
            to(slot, slot, cot_ss.at[block], cot_rs.at[block], src_at=block).wait_recv()
        light = cbuf[block]
        backs = []
        for one in range(per_device):
            real = fbuf[block, one * local_x : (one + 1) * local_x, :pixels]
            imag = fbuf[block, one * local_x : (one + 1) * local_x, pixels:]
            lit_real, lit_imag = light * real, light * imag
            scale = 2.0 * weights[one]
            backs.append(jnp.concatenate([scale * lit_real, scale * lit_imag], axis=1))
            terms[one] = terms[one] + jnp.sum(
                lit_real * real + lit_imag * imag, axis=0, keepdims=True
            )
        adjoint = dot_pair(pair(jnp.concatenate(backs, axis=0)), wy, 1)
        for one in range(per_device):
            rows = slice(one * local_x, (one + 1) * local_x)
            cols = slice(one * freqs, (one + 1) * freqs)
            ubuf[block, :, cols] = adjoint[rows, :freqs]
            ubuf[src_count + block, :, cols] = adjoint[rows, freqs:]

    term_send[...] = jnp.zeros(term_send.shape, jnp.float32)
    for one in range(per_device):
        term_send[one : one + 1, :] = terms[one][:, :freqs] + terms[one][:, freqs:]
    for index, (src_at, tile_at, row_at) in enumerate(near):
        copy = to(
            term_send,
            term_recv.at[index],
            term_ss.at[index],
            term_rs.at[index],
            tile_at=tile_at,
            row_at=row_at,
        )
        copy.start()
        copies.append(copy)

    wx = (wx_ref[0], wx_ref[1])
    swept = ubuf[...].reshape(2 * src_count * local_x, per_device * freqs)
    swept = dot_pair(wx, pair(swept)) * field_scale
    grad_real = jnp.zeros((freqs, freqs), jnp.float32)
    grad_imag = grad_real
    for one, (pr, pi) in enumerate(pupils):
        cols = slice(one * freqs, (one + 1) * freqs)
        real, imag = swept[:freqs, cols], swept[freqs:, cols]
        grad_real = grad_real + pr * real + pi * imag
        grad_imag = grad_imag + pr * imag - pi * real
    grads = pair(jnp.concatenate([grad_real, grad_imag], axis=0))

    def rows_of(index):
        swept = dot_pair((wxt_ref[0, index], wxt_ref[1, index]), grads)
        half = src_count * local_x
        swept = jnp.concatenate([swept[:half], swept[half:]], axis=1)
        return swept.reshape(src_count, local_x, 2 * freqs)

    core_send[...] = rows_of(other_row)
    core_copy = to(core_send, core_recv, core_ss, core_rs, row_at=other_row)
    core_copy.start()
    copies.append(core_copy)
    grad_send[...] = rows_of(row)
    core_copy.wait_recv()
    for peer in far_first:
        grad_send[peer] = grad_send[peer] + core_recv[peer]
        copy = to(
            grad_send.at[peer],
            grad_recv.at[src],
            grad_ss.at[peer],
            grad_rs.at[src],
            src_at=peer,
        )
        copy.start()
        copies.append(copy)
    grad_send[src] = grad_send[src] + core_recv[src]

    lanes = lax.broadcasted_iota(jnp.int32, (local_x, freqs), 1)
    edge_wave = tuple(
        jnp.where(
            tile == 0,
            wy_ref[index, :, pixels - freqs : pixels].astype(jnp.float32),
            wy_ref[index, :, :freqs].astype(jnp.float32),
        ).astype(jnp.bfloat16)
        for index in range(2)
    )
    edges = grad_send[...].reshape(src_count * local_x, 2 * freqs)
    edges = dot_pair(pair(edges), edge_wave).reshape(src_count, local_x, freqs)
    fold = freqs // OV
    depth = local_x // fold
    for block in range(src_count):
        strip = jnp.where(tile == 0, pltpu.roll(edges[block], OV, axis=1), edges[block])
        strip = jnp.where(lanes < OV, strip, 0.0)
        packed = strip[:depth]
        for one in range(1, fold):
            packed = packed + pltpu.roll(
                strip[one * depth : (one + 1) * depth], one * OV, axis=1
            )
        halo_send[block] = packed
    for peer in far_first + [src]:
        copy = to(
            halo_send.at[peer],
            halo_recv.at[src],
            halo_ss.at[peer],
            halo_rs.at[src],
            src_at=peer,
            tile_at=other_tile,
        )
        copy.start()
        copies.append(copy)

    for index, (src_at, tile_at, row_at) in enumerate(near):
        to(
            term_send,
            term_recv.at[index],
            term_ss.at[index],
            term_rs.at[index],
            tile_at=tile_at,
            row_at=row_at,
        ).wait_recv()
    total = (term_send[...] + term_recv[0]) + (term_recv[1] + term_recv[2])
    total = total / (sources * pixels * tile_count)
    for one in range(per_device):
        terms_ref[one] = jnp.sum(total[one : one + 1, :])

    total = grad_send[src]
    for peer in near_first:
        to(
            grad_send.at[peer],
            grad_recv.at[peer],
            grad_ss.at[peer],
            grad_rs.at[peer],
            src_at=peer,
        ).wait_recv()
        total = total + grad_recv[peer]
    grad_block = dot_pair(pair(total), wf)
    low, high = grad_block[:, :freqs], grad_block[:, pixels - freqs :]

    packed = jnp.zeros((depth, freqs), jnp.float32)
    for peer in [src] + near_first:
        to(
            halo_send.at[peer],
            halo_recv.at[peer],
            halo_ss.at[peer],
            halo_rs.at[peer],
            src_at=peer,
            tile_at=other_tile,
        ).wait_recv()
        packed = packed + halo_recv[peer]
    strip = jnp.concatenate(
        [packed]
        + [pltpu.roll(packed, freqs - one * OV, axis=1) for one in range(1, fold)],
        axis=0,
    )
    from_below = jnp.where((lanes < OV) & (tile == 1), strip, 0.0)
    from_above = jnp.where(
        (lanes >= freqs - OV) & (tile == 0), pltpu.roll(strip, freqs - OV, axis=1), 0.0
    )
    out_ref[0, :, :freqs] = low + from_below
    out_ref[0, :, pixels - freqs :] = high + from_above
    for copy in copies:
        copy.wait_send()


def shards(mask_windows, target_windows, pupil_bands, pupil_phase, source_weight):
    src_count = lax.axis_size("src")
    tile_count = lax.axis_size("tile")
    row_count = lax.axis_size("row")
    local_x, pixels = mask_windows.shape[1:]
    per_device, freqs = pupil_phase.shape[:2]
    fits = row_count == 2 and tile_count == 2 and src_count > 1
    if not fits or local_x % 32 != 0 or freqs % 128 != 0 or pixels != 2 * freqs or OV != 32:
        return shards_plain(
            mask_windows, target_windows, pupil_bands, pupil_phase, source_weight
        )
    tables = [
        split_constant(one)
        for one in wave_constants(pixels, freqs, src_count, row_count, local_x)
    ]
    bands = jnp.transpose(pupil_bands, (0, 2, 1))
    in_vmem = pl.BlockSpec(memory_space=pltpu.VMEM)
    in_smem = pl.BlockSpec(memory_space=pltpu.SMEM)
    f32 = jnp.float32
    block = (local_x, pixels)
    dma = pltpu.SemaphoreType.DMA
    return pl.pallas_call(
        functools.partial(kernel, src_count, row_count, tile_count),
        out_shape=(
            jax.ShapeDtypeStruct(mask_windows.shape, f32),
            jax.ShapeDtypeStruct(source_weight.shape, f32),
        ),
        in_specs=[pl.BlockSpec(memory_space=pltpu.HBM)] * 8,
        out_specs=(in_vmem, in_smem),
        scratch_shapes=[
            pltpu.VMEM(tables[0].shape, tables[0].dtype),
            pltpu.VMEM(tables[1].shape[:1] + tables[1].shape[2:], tables[1].dtype),
            pltpu.VMEM(tables[2].shape, tables[2].dtype),
            pltpu.VMEM(mask_windows.shape, f32),
            pltpu.VMEM(target_windows.shape, f32),
            pltpu.VMEM(bands.shape, bands.dtype),
            pltpu.VMEM(pupil_phase.shape, f32),
            pltpu.SMEM(source_weight.shape, f32),
            dma((8,)),
            pltpu.VMEM((src_count * row_count,) + block, f32),
            pltpu.VMEM((2 * src_count, local_x, per_device * freqs), f32),
            pltpu.VMEM((src_count, per_device * local_x, 2 * pixels), f32),
            pltpu.VMEM((2 * src_count, local_x, per_device * freqs), f32),
        ]
        + [pltpu.VMEM((src_count,) + block, f32)] * 7
        + [
            pltpu.VMEM((src_count, local_x * OV // freqs, freqs), f32),
            pltpu.VMEM((src_count, local_x * OV // freqs, freqs), f32),
            pltpu.VMEM((8, freqs), f32),
            pltpu.VMEM((3, 8, freqs), f32),
        ]
        + [dma((src_count,))] * 8
        + [dma(()), dma(())]
        + [dma((src_count,))] * 4
        + [dma((3,))] * 2,
        compiler_params=pltpu.CompilerParams(
            collective_id=0, has_side_effects=True, vmem_limit_bytes=63 * 1024 * 1024
        ),
    )(*tables, mask_windows, target_windows, bands, pupil_phase, source_weight)


def solution(mesh):
    return jax.shard_map(
        shards,
        mesh=mesh,
        in_specs=(
            P(("parts", "tile"), ("src", "row"), None),
            P(("parts", "tile"), ("src", "row"), None),
            P(("parts", "src"), None, None),
            P(("parts", "src"), None, None),
            P(("parts", "src")),
        ),
        out_specs=(P(("parts", "tile"), ("src", "row"), None), P(("parts", "src"))),
        check_vma=False,
    )
```

```python
import functools
import math

import jax
import jax.numpy as jnp
import numpy as np
from jax import lax
from jax.experimental import pallas as pl
from jax.experimental.pallas import tpu as pltpu
from jax.sharding import PartitionSpec as P

M = 256
K = 128
OV = 32


STEEPNESS = 20.0
THRESHOLD = 0.15
LOSS_SCALE = 32.0


def with_halo(block, sides, width):
    for axis, dim in sides:
        count = lax.axis_size(axis)
        forward = [(i, i + 1) for i in range(count - 1)]
        backward = [(target, source) for source, target in forward]
        low = lax.ppermute(
            lax.slice_in_dim(block, block.shape[dim] - width, None, axis=dim), axis, forward
        )
        high = lax.ppermute(lax.slice_in_dim(block, 0, width, axis=dim), axis, backward)
        block = jnp.concatenate([low, block, high], axis=dim)
    return block


def matmul(left_op, right_op):
    return lax.dot_general(
        left_op,
        right_op,
        (((1,), (0,)), ((), ())),
        precision=lax.Precision.HIGHEST,
        preferred_element_type=jnp.float32,
    )


def matmul_tn(left_op, right_op):
    return lax.dot_general(
        left_op,
        right_op,
        (((0,), (0,)), ((), ())),
        precision=lax.Precision.HIGHEST,
        preferred_element_type=jnp.float32,
    )


def matmul_nt(left_op, right_op):
    return lax.dot_general(
        left_op,
        right_op,
        (((1,), (1,)), ((), ())),
        precision=lax.Precision.HIGHEST,
        preferred_element_type=jnp.float32,
    )


def wave_tables(positions):
    freq_index = jnp.arange(K, dtype=jnp.int32) - K // 2
    phase_index = freq_index[:, None] * positions[None, :] % M
    angles = 2.0 * math.pi / M * phase_index.astype(jnp.float32)
    return (jnp.cos(angles), jnp.sin(angles))


def shards_plain(mask_windows, target_windows, pupil_bands, pupil_phase, source_weight):
    src_count = lax.axis_size("src")
    tile_count = lax.axis_size("tile")
    row_count = lax.axis_size("row")
    local_x = mask_windows.shape[1]
    per_device = pupil_phase.shape[0]
    sources = per_device * src_count
    field_scale = 1.0 / (M * K)
    src_id = lax.axis_index("src")
    row_id = lax.axis_index("row")
    x_start = (src_id * row_count + row_id) * local_x
    block_starts = (jnp.arange(src_count, dtype=jnp.int32) * row_count + row_id) * local_x
    row_set = (block_starts[:, None] + jnp.arange(local_x, dtype=jnp.int32)[None, :]).reshape(
        src_count * local_x
    )
    cos_all, sin_all = wave_tables(jnp.arange(M, dtype=jnp.int32))
    cos_set, sin_set = wave_tables(row_set)
    cos_own, sin_own = wave_tables(x_start + jnp.arange(local_x, dtype=jnp.int32))
    window = mask_windows[0]
    goal_block = target_windows[0]
    zero_spec = jnp.zeros((K, K), jnp.float32)
    shard_rows = lax.all_gather(window, ("src", "row"), axis=0, tiled=True)
    part_real = matmul_nt(shard_rows, cos_all)
    part_imag = -matmul_nt(shard_rows, sin_all)
    spec_real = matmul(cos_all, part_real) + matmul(sin_all, part_imag)
    spec_imag = matmul(cos_all, part_imag) - matmul(sin_all, part_real)
    freq_cols = jnp.arange(K, dtype=jnp.int32)
    inside = (freq_cols[None, None, :] >= pupil_bands[:, :, 0:1]) & (
        freq_cols[None, None, :] < pupil_bands[:, :, 1:2]
    )
    passing = inside.astype(jnp.float32)
    pupil_real = passing * jnp.cos(pupil_phase)
    pupil_imag = passing * jnp.sin(pupil_phase)
    amp_real = (pupil_real * spec_real - pupil_imag * spec_imag).reshape(per_device * K, K)
    amp_imag = (pupil_imag * spec_real + pupil_real * spec_imag).reshape(per_device * K, K)
    half_real = (matmul(amp_real, cos_all) - matmul(amp_imag, sin_all)).reshape(per_device, K, M)
    half_imag = (matmul(amp_real, sin_all) + matmul(amp_imag, cos_all)).reshape(per_device, K, M)
    weights = source_weight / sources

    def fields(pair_in):
        one_real, one_imag = pair_in
        field_real = field_scale * (matmul_tn(cos_set, one_real) - matmul_tn(sin_set, one_imag))
        field_imag = field_scale * (matmul_tn(cos_set, one_imag) + matmul_tn(sin_set, one_real))
        return (field_real, field_imag)

    stack_real, stack_imag = lax.map(fields, (half_real, half_imag))
    part_real = stack_real
    part_imag = stack_imag
    intensity = lax.psum_scatter(
        jnp.sum(weights[:, None, None] * (part_real * part_real + part_imag * part_imag), axis=0),
        "src",
        scatter_dimension=0,
        tiled=True,
    )
    resist = jax.nn.sigmoid(STEEPNESS * (intensity - THRESHOLD))
    cotangent = LOSS_SCALE * (resist - goal_block) * STEEPNESS * resist * (1.0 - resist)
    cotangent_all = lax.all_gather(cotangent, "src", axis=0, tiled=True)
    source_ids = jnp.arange(per_device, dtype=jnp.int32)

    def add_back(source_id, totals):
        grad_real, grad_imag, source_terms = totals
        field_real = stack_real[source_id]
        field_imag = stack_imag[source_id]
        back_scale = 2.0 * weights[source_id] * cotangent_all
        back_real = back_scale * field_real
        back_imag = back_scale * field_imag
        adj_real = matmul(cos_set, back_real) + matmul(sin_set, back_imag)
        adj_imag = matmul(cos_set, back_imag) - matmul(sin_set, back_real)
        amp_grad_real = field_scale * (matmul_nt(adj_real, cos_all) + matmul_nt(adj_imag, sin_all))
        amp_grad_imag = field_scale * (matmul_nt(adj_imag, cos_all) - matmul_nt(adj_real, sin_all))
        pass_real = pupil_real[source_id]
        pass_imag = pupil_imag[source_id]
        grad_real = grad_real + pass_real * amp_grad_real + pass_imag * amp_grad_imag
        grad_imag = grad_imag + pass_real * amp_grad_imag - pass_imag * amp_grad_real
        term_value = jnp.sum(cotangent_all * (field_real * field_real + field_imag * field_imag))
        source_terms = source_terms + jnp.where(source_ids == source_id, term_value, 0.0)
        return (grad_real, grad_imag, source_terms)

    grad_real, grad_imag, source_terms = lax.fori_loop(
        0, per_device, add_back, (zero_spec, zero_spec, jnp.zeros((per_device,), jnp.float32))
    )
    grad_real, grad_imag = lax.psum((grad_real, grad_imag), ("src", "row"))
    source_sum = lax.psum(source_terms, ("tile", "row"))
    source_grad = source_sum / (sources * M * tile_count)
    q_one = matmul(grad_real, cos_all) - matmul(grad_imag, sin_all)
    q_two = matmul(grad_real, sin_all) + matmul(grad_imag, cos_all)
    grad_block = matmul_tn(cos_own, q_one) - matmul_tn(sin_own, q_two)
    padded = with_halo(grad_block, (("tile", 1),), OV)
    from_below = padded[:, :OV]
    from_above = padded[:, M + OV :]
    middle = jnp.zeros((local_x, M - 2 * OV), jnp.float32)
    grad_block = grad_block + jnp.concatenate([from_below, middle, from_above], axis=1)
    return (grad_block[None], source_grad)


MESH = pl.DeviceIdType.MESH


def pair(values):
    high = values.astype(jnp.bfloat16)
    return high, (values - high.astype(jnp.float32)).astype(jnp.bfloat16)


def dot_pair(left_op, right_op, contract_right=0):
    dims = (((1,), (contract_right,)), ((), ()))

    def one(a, b):
        return lax.dot_general(a, b, dims, preferred_element_type=jnp.float32)

    (left_high, left_low), (right_high, right_low) = left_op, right_op
    return one(left_high, right_high) + (
        one(left_high, right_low) + one(left_low, right_high)
    )


def wave_constants(pixels, freqs, src_count, row_count, local_x):
    freq_index = np.arange(freqs) - freqs // 2
    angles = 2.0 * np.pi / pixels * (np.outer(freq_index, np.arange(pixels)) % pixels)
    cos_tab, sin_tab = np.cos(angles), np.sin(angles)
    wave_y = np.block([[cos_tab, sin_tab], [-sin_tab, cos_tab]])
    sets = []
    for row in range(row_count):
        starts = (np.arange(src_count) * row_count + row) * local_x
        rows = (starts[:, None] + np.arange(local_x)[None, :]).reshape(-1)
        c, s = cos_tab[:, rows], sin_tab[:, rows]
        sets.append(np.block([[c, s], [-s, c]]))
    wave_x = np.stack(sets)
    return wave_y, wave_x, np.ascontiguousarray(wave_x.transpose(0, 2, 1))


def split_constant(values):
    values = values.astype(np.float32)
    high = values.astype(jnp.bfloat16)
    low = (values - high.astype(np.float32)).astype(jnp.bfloat16)
    return np.stack([high, low])


def kernel(
    src_count,
    row_count,
    tile_count,
    wy_hbm,
    wx_hbm,
    wxt_hbm,
    mask_hbm,
    goal_hbm,
    band_hbm,
    phase_hbm,
    weight_hbm,
    out_ref,
    terms_ref,
    wy_ref,
    wx_ref,
    wxt_ref,
    mask_ref,
    goal_ref,
    band_ref,
    phase_ref,
    weight_ref,
    load_sems,
    pbuf,
    tbuf,
    fbuf,
    ubuf,
    part_send,
    part_recv,
    cbuf,
    core_send,
    core_recv,
    grad_send,
    grad_recv,
    halo_send,
    halo_recv,
    term_send,
    term_recv,
    mask_ss,
    mask_rs,
    fwd_ss,
    fwd_rs,
    part_ss,
    part_rs,
    cot_ss,
    cot_rs,
    core_ss,
    core_rs,
    grad_ss,
    grad_rs,
    halo_ss,
    halo_rs,
    term_ss,
    term_rs,
):
    part = lax.axis_index("parts")
    src = lax.axis_index("src")
    tile = lax.axis_index("tile")
    row = lax.axis_index("row")
    local_x, pixels = mask_ref.shape[1:]
    per_device, freqs = phase_ref.shape[:2]
    sources = per_device * src_count
    field_scale = 1.0 / (pixels * freqs)
    loads = {}
    for index, (name, source, target) in enumerate(
        [
            ("mask", mask_hbm, mask_ref),
            ("wy", wy_hbm, wy_ref),
            ("phase", phase_hbm, phase_ref),
            ("band", band_hbm, band_ref),
            ("wxt", wxt_hbm, wxt_ref),
            ("weight", weight_hbm, weight_ref),
            ("goal", goal_hbm, goal_ref),
            ("wx", wx_hbm.at[:, row], wx_ref),
        ]
    ):
        loads[name] = pltpu.make_async_copy(source, target, load_sems.at[index])
        loads[name].start()
    other_row = 1 - row
    other_tile = 1 - tile
    last = src_count - 1

    def far(step):
        up = last - src
        side = lax.div(up + last - step, src_count)
        return side * (last - step) + (1 - side) * (step - up)

    far_first = [far(step) for step in range(last)]
    near_first = far_first[::-1]

    def to(src_ref, dst_ref, ss, rs, src_at=src, tile_at=tile, row_at=row):
        return pltpu.make_async_remote_copy(
            src_ref=src_ref,
            dst_ref=dst_ref,
            send_sem=ss,
            recv_sem=rs,
            device_id=(part, src_at, tile_at, row_at),
            device_id_type=MESH,
        )

    barrier = pltpu.get_barrier_semaphore()
    near = [(src, tile, other_row), (src, other_tile, row), (src, other_tile, other_row)]
    peers = [(peer, tile, row) for peer in far_first] + near
    for src_at, tile_at, row_at in peers:
        pl.semaphore_signal(
            barrier, inc=1, device_id=(part, src_at, tile_at, row_at), device_id_type=MESH
        )

    loads["mask"].wait()
    loads["wy"].wait()
    wy = (wy_ref[0], wy_ref[1])
    wf = (wy_ref[0, :, :pixels], wy_ref[1, :, :pixels])
    own_slot = src * row_count + row
    pbuf[own_slot] = dot_pair(pair(mask_ref[0]), wf, 1)
    pl.semaphore_wait(barrier, len(peers))

    own_block = pbuf.at[own_slot]
    copies = []
    for peer in far_first:
        copy = to(own_block, own_block, mask_ss.at[peer], mask_rs.at[src], src_at=peer)
        copy.start()
        copies.append(copy)
    copy = to(own_block, own_block, fwd_ss.at[src], fwd_rs.at[src], row_at=other_row)
    copy.start()
    copies.append(copy)

    loads["phase"].wait()
    loads["band"].wait()
    freq_rows = lax.broadcasted_iota(jnp.int32, (freqs, freqs), 0)
    pupils = []
    for one in range(per_device):
        inside = (freq_rows >= band_ref[one, 0:1, :]) & (freq_rows < band_ref[one, 1:2, :])
        passing = jnp.where(inside, 1.0, 0.0).T
        phase = phase_ref[one]
        pupils.append((passing * jnp.cos(phase), passing * jnp.sin(phase)))

    for name in ("wxt", "weight", "goal", "wx"):
        loads[name].wait()
    for peer in near_first:
        block = pbuf.at[peer * row_count + row]
        to(block, block, mask_ss.at[peer], mask_rs.at[peer], src_at=peer).wait_recv()
        copy = to(block, block, fwd_ss.at[peer], fwd_rs.at[peer], row_at=other_row)
        copy.start()
        copies.append(copy)
    for peer in [src] + near_first:
        block = pbuf.at[peer * row_count + other_row]
        to(block, block, fwd_ss.at[peer], fwd_rs.at[peer], row_at=other_row).wait_recv()

    columns = pair(pbuf[...].reshape(pixels, pixels))
    spectrum = dot_pair(wf, columns)
    spec_real = spectrum[:freqs, :freqs] - spectrum[freqs:, freqs:]
    spec_imag = spectrum[:freqs, freqs:] + spectrum[freqs:, :freqs]

    amps = jnp.concatenate(
        [
            jnp.concatenate([pr * spec_real - pi * spec_imag for pr, pi in pupils], axis=1),
            jnp.concatenate([pi * spec_real + pr * spec_imag for pr, pi in pupils], axis=1),
        ],
        axis=0,
    )
    wxt = (wxt_ref[0, row], wxt_ref[1, row])
    swept = dot_pair(wxt, pair(amps)) * field_scale
    tbuf[...] = swept.reshape(2 * src_count, local_x, per_device * freqs)

    weights = [weight_ref[one] / sources for one in range(per_device)]
    for block in far_first + [src]:
        real, imag = tbuf[block], tbuf[src_count + block]
        rows = jnp.concatenate(
            [
                jnp.concatenate(
                    [
                        real[:, one * freqs : (one + 1) * freqs],
                        imag[:, one * freqs : (one + 1) * freqs],
                    ],
                    axis=1,
                )
                for one in range(per_device)
            ],
            axis=0,
        )
        field = dot_pair(pair(rows), wy)
        fbuf[block] = field
        squares = field[:, :pixels] * field[:, :pixels] + field[:, pixels:] * field[:, pixels:]
        total = weights[0] * squares[:local_x]
        for one in range(1, per_device):
            total = total + weights[one] * squares[one * local_x : (one + 1) * local_x]
        if block is not src:
            part_send[block] = total
            copy = to(
                part_send.at[block],
                part_recv.at[src],
                part_ss.at[block],
                part_rs.at[src],
                src_at=block,
            )
            copy.start()
            copies.append(copy)

    intensity = total
    for peer in near_first:
        to(
            part_send.at[peer],
            part_recv.at[peer],
            part_ss.at[peer],
            part_rs.at[peer],
            src_at=peer,
        ).wait_recv()
        intensity = intensity + part_recv[peer]

    resist = 1.0 / (1.0 + jnp.exp(-STEEPNESS * (intensity - THRESHOLD)))
    cotangent = LOSS_SCALE * (resist - goal_ref[0]) * STEEPNESS * resist * (1.0 - resist)
    cbuf[src] = cotangent
    for peer in far_first:
        block = cbuf.at[src]
        copy = to(block, block, cot_ss.at[peer], cot_rs.at[src], src_at=peer)
        copy.start()
        copies.append(copy)

    terms = [jnp.zeros((1, pixels), jnp.float32)] * per_device
    for block in [src] + near_first:
        if block is not src:
            slot = cbuf.at[block]
            to(slot, slot, cot_ss.at[block], cot_rs.at[block], src_at=block).wait_recv()
        light = cbuf[block]
        backs = []
        for one in range(per_device):
            real = fbuf[block, one * local_x : (one + 1) * local_x, :pixels]
            imag = fbuf[block, one * local_x : (one + 1) * local_x, pixels:]
            lit_real, lit_imag = light * real, light * imag
            scale = 2.0 * weights[one]
            backs.append(jnp.concatenate([scale * lit_real, scale * lit_imag], axis=1))
            terms[one] = terms[one] + jnp.sum(
                lit_real * real + lit_imag * imag, axis=0, keepdims=True
            )
        adjoint = dot_pair(pair(jnp.concatenate(backs, axis=0)), wy, 1)
        for one in range(per_device):
            rows = slice(one * local_x, (one + 1) * local_x)
            cols = slice(one * freqs, (one + 1) * freqs)
            ubuf[block, :, cols] = adjoint[rows, :freqs]
            ubuf[src_count + block, :, cols] = adjoint[rows, freqs:]

    term_send[...] = jnp.zeros(term_send.shape, jnp.float32)
    for one in range(per_device):
        term_send[one : one + 1, :] = terms[one][:, :freqs] + terms[one][:, freqs:]
    for index, (src_at, tile_at, row_at) in enumerate(near):
        copy = to(
            term_send,
            term_recv.at[index],
            term_ss.at[index],
            term_rs.at[index],
            tile_at=tile_at,
            row_at=row_at,
        )
        copy.start()
        copies.append(copy)

    wx = (wx_ref[0], wx_ref[1])
    swept = ubuf[...].reshape(2 * src_count * local_x, per_device * freqs)
    swept = dot_pair(wx, pair(swept)) * field_scale
    grad_real = jnp.zeros((freqs, freqs), jnp.float32)
    grad_imag = grad_real
    for one, (pr, pi) in enumerate(pupils):
        cols = slice(one * freqs, (one + 1) * freqs)
        real, imag = swept[:freqs, cols], swept[freqs:, cols]
        grad_real = grad_real + pr * real + pi * imag
        grad_imag = grad_imag + pr * imag - pi * real
    grads = pair(jnp.concatenate([grad_real, grad_imag], axis=0))

    def rows_of(index):
        swept = dot_pair((wxt_ref[0, index], wxt_ref[1, index]), grads)
        half = src_count * local_x
        swept = jnp.concatenate([swept[:half], swept[half:]], axis=1)
        return swept.reshape(src_count, local_x, 2 * freqs)

    core_send[...] = rows_of(other_row)
    core_copy = to(core_send, core_recv, core_ss, core_rs, row_at=other_row)
    core_copy.start()
    copies.append(core_copy)
    grad_send[...] = rows_of(row)
    core_copy.wait_recv()
    for peer in far_first:
        grad_send[peer] = grad_send[peer] + core_recv[peer]
        copy = to(
            grad_send.at[peer],
            grad_recv.at[src],
            grad_ss.at[peer],
            grad_rs.at[src],
            src_at=peer,
        )
        copy.start()
        copies.append(copy)
    grad_send[src] = grad_send[src] + core_recv[src]

    lanes = lax.broadcasted_iota(jnp.int32, (local_x, freqs), 1)
    edge_wave = tuple(
        jnp.where(
            tile == 0,
            wy_ref[index, :, pixels - freqs : pixels].astype(jnp.float32),
            wy_ref[index, :, :freqs].astype(jnp.float32),
        ).astype(jnp.bfloat16)
        for index in range(2)
    )
    edges = grad_send[...].reshape(src_count * local_x, 2 * freqs)
    edges = dot_pair(pair(edges), edge_wave).reshape(src_count, local_x, freqs)
    fold = freqs // OV
    depth = local_x // fold
    for block in range(src_count):
        strip = jnp.where(tile == 0, pltpu.roll(edges[block], OV, axis=1), edges[block])
        strip = jnp.where(lanes < OV, strip, 0.0)
        packed = strip[:depth]
        for one in range(1, fold):
            packed = packed + pltpu.roll(
                strip[one * depth : (one + 1) * depth], one * OV, axis=1
            )
        halo_send[block] = packed
    for peer in far_first + [src]:
        copy = to(
            halo_send.at[peer],
            halo_recv.at[src],
            halo_ss.at[peer],
            halo_rs.at[src],
            src_at=peer,
            tile_at=other_tile,
        )
        copy.start()
        copies.append(copy)

    for index, (src_at, tile_at, row_at) in enumerate(near):
        to(
            term_send,
            term_recv.at[index],
            term_ss.at[index],
            term_rs.at[index],
            tile_at=tile_at,
            row_at=row_at,
        ).wait_recv()
    total = (term_send[...] + term_recv[0]) + (term_recv[1] + term_recv[2])
    total = total / (sources * pixels * tile_count)
    for one in range(per_device):
        terms_ref[one] = jnp.sum(total[one : one + 1, :])

    total = grad_send[src]
    for peer in near_first:
        to(
            grad_send.at[peer],
            grad_recv.at[peer],
            grad_ss.at[peer],
            grad_rs.at[peer],
            src_at=peer,
        ).wait_recv()
        total = total + grad_recv[peer]
    grad_block = dot_pair(pair(total), wf)
    low, high = grad_block[:, :freqs], grad_block[:, pixels - freqs :]

    packed = jnp.zeros((depth, freqs), jnp.float32)
    for peer in [src] + near_first:
        to(
            halo_send.at[peer],
            halo_recv.at[peer],
            halo_ss.at[peer],
            halo_rs.at[peer],
            src_at=peer,
            tile_at=other_tile,
        ).wait_recv()
        packed = packed + halo_recv[peer]
    strip = jnp.concatenate(
        [packed]
        + [pltpu.roll(packed, freqs - one * OV, axis=1) for one in range(1, fold)],
        axis=0,
    )
    from_below = jnp.where((lanes < OV) & (tile == 1), strip, 0.0)
    from_above = jnp.where(
        (lanes >= freqs - OV) & (tile == 0), pltpu.roll(strip, freqs - OV, axis=1), 0.0
    )
    out_ref[0, :, :freqs] = low + from_below
    out_ref[0, :, pixels - freqs :] = high + from_above
    for copy in copies:
        copy.wait_send()


def shards(mask_windows, target_windows, pupil_bands, pupil_phase, source_weight):
    src_count = lax.axis_size("src")
    tile_count = lax.axis_size("tile")
    row_count = lax.axis_size("row")
    local_x, pixels = mask_windows.shape[1:]
    per_device, freqs = pupil_phase.shape[:2]
    fits = row_count == 2 and tile_count == 2 and src_count > 1
    if not fits or local_x % 32 != 0 or freqs % 128 != 0 or pixels != 2 * freqs or OV != 32:
        return shards_plain(
            mask_windows, target_windows, pupil_bands, pupil_phase, source_weight
        )
    tables = [
        split_constant(one)
        for one in wave_constants(pixels, freqs, src_count, row_count, local_x)
    ]
    bands = jnp.transpose(pupil_bands, (0, 2, 1))
    in_vmem = pl.BlockSpec(memory_space=pltpu.VMEM)
    in_smem = pl.BlockSpec(memory_space=pltpu.SMEM)
    f32 = jnp.float32
    block = (local_x, pixels)
    dma = pltpu.SemaphoreType.DMA
    return pl.pallas_call(
        functools.partial(kernel, src_count, row_count, tile_count),
        out_shape=(
            jax.ShapeDtypeStruct(mask_windows.shape, f32),
            jax.ShapeDtypeStruct(source_weight.shape, f32),
        ),
        in_specs=[pl.BlockSpec(memory_space=pltpu.HBM)] * 8,
        out_specs=(in_vmem, in_smem),
        scratch_shapes=[
            pltpu.VMEM(tables[0].shape, tables[0].dtype),
            pltpu.VMEM(tables[1].shape[:1] + tables[1].shape[2:], tables[1].dtype),
            pltpu.VMEM(tables[2].shape, tables[2].dtype),
            pltpu.VMEM(mask_windows.shape, f32),
            pltpu.VMEM(target_windows.shape, f32),
            pltpu.VMEM(bands.shape, bands.dtype),
            pltpu.VMEM(pupil_phase.shape, f32),
            pltpu.SMEM(source_weight.shape, f32),
            dma((8,)),
            pltpu.VMEM((src_count * row_count,) + block, f32),
            pltpu.VMEM((2 * src_count, local_x, per_device * freqs), f32),
            pltpu.VMEM((src_count, per_device * local_x, 2 * pixels), f32),
            pltpu.VMEM((2 * src_count, local_x, per_device * freqs), f32),
        ]
        + [pltpu.VMEM((src_count,) + block, f32)] * 7
        + [
            pltpu.VMEM((src_count, local_x * OV // freqs, freqs), f32),
            pltpu.VMEM((src_count, local_x * OV // freqs, freqs), f32),
            pltpu.VMEM((8, freqs), f32),
            pltpu.VMEM((3, 8, freqs), f32),
        ]
        + [dma((src_count,))] * 8
        + [dma(()), dma(())]
        + [dma((src_count,))] * 4
        + [dma((3,))] * 2,
        compiler_params=pltpu.CompilerParams(
            collective_id=0, has_side_effects=True, vmem_limit_bytes=63 * 1024 * 1024
        ),
    )(*tables, mask_windows, target_windows, bands, pupil_phase, source_weight)


def solution(mesh):
    return jax.shard_map(
        shards,
        mesh=mesh,
        in_specs=(
            P(("parts", "tile"), ("src", "row"), None),
            P(("parts", "tile"), ("src", "row"), None),
            P(("parts", "src"), None, None),
            P(("parts", "src"), None, None),
            P(("parts", "src")),
        ),
        out_specs=(P(("parts", "tile"), ("src", "row"), None), P(("parts", "src"))),
        check_vma=False,
    )
```
